32 devices in a mesh: groups: 2 (over x), refl: 8 (over z, y), freq: 2 (over core).
Axes of the slice: x: 2, y: 2, z: 4, core: 2. Of those that a mesh axis runs over, the one named last changes fastest.
Arguments:
- spectra: bfloat16 [2, 16, 1024, 8192], P(None, 'freq', 'groups', 'refl'), parts along dimension 2, may hold values from -9 to 9
- recorded: bfloat16 [8, 2, 64, 64, 256], P('refl', 'freq', 'groups'), parts along dimension 2, may hold values from -10 to 10
- initial_filters: float32 [8, 2, 2, 2, 33], P('refl', 'freq', 'groups'), parts along dimension 2, may hold values from -0.6 to 0.6
Outputs:
- primaries: bfloat16 [8, 2, 64, 64, 256], P('refl', 'freq', 'groups'), parts along dimension 2
- filters: float32 [8, 2, 2, 2, 33], P('refl', 'freq', 'groups'), parts along dimension 2
The draws below stay inside these ranges and needn't reach their ends.
There are 2 independent parts, one for each index of `groups`. The reference program is written for one: setup_inputs(seed, part) draws one part's arguments, and reference() takes and returns one part's arrays. A program takes and returns all parts, laid end to end along the dimension named above; each array names one. Nothing has to cross between parts.
All inputs are finite; a program needn't handle non-finite values.
Results may differ from the reference program's by a relative error of at most 0.025.
Values may be sent and summed in bfloat16 or wider, within the bound.
A program may use at most 128 MiB of HBM per device.

```python
import math
import jax
import jax.numpy as jnp
from jax import lax

NF = 16
K0 = 48
NT = 256
XR = 8192
TS = 32
TR = 64
WC = 32
WM = 4
TAPS = 33
ITERS = 3
FB = 2
ST = 2
NS = 64
NR = 512
N_REFL = 8
N_FREQ = 2


def make_spectra(key):
    noise_key, scale_key = jax.random.split(jax.random.fold_in(key, 17))
    noise = jax.random.truncated_normal(noise_key, -3.0, 3.0, (2, NF, NR, XR), jnp.float32)
    spread = jnp.exp(jax.random.uniform(scale_key, (1, 1, NR, 1), jnp.float32, 0.0, math.log(8.0))) / 2.8
    return (noise * spread).astype(jnp.bfloat16)


def draw_spectra(key, part):
    return make_spectra(key)


def predicted_traces(key):
    spectra = make_spectra(key).astype(jnp.float32)
    real_full = spectra[0]
    imaginary_full = spectra[1]
    block_width = math.gcd(XR, 256)
    block_count = XR // block_width
    amplitude = 1.0 / math.sqrt(2.0 * XR)
    highest_precision = lax.Precision.HIGHEST

    def add_block(block_index, running):
        real_totals, imaginary_totals = running
        first_point = (block_index * block_width).astype(jnp.int32)
        real_block_piece = lax.dynamic_slice_in_dim(real_full, first_point, block_width, 2)
        imaginary_block_piece = lax.dynamic_slice_in_dim(imaginary_full, first_point, block_width, 2)
        real_source_rows = real_block_piece[:, :NS]
        imaginary_source_rows = imaginary_block_piece[:, :NS]
        real_portion = jnp.einsum('hvt,hkt->hvk', real_source_rows, real_block_piece, precision=highest_precision) - jnp.einsum('hvt,hkt->hvk', imaginary_source_rows, imaginary_block_piece, precision=highest_precision)
        imaginary_portion = jnp.einsum('hvt,hkt->hvk', real_source_rows, imaginary_block_piece, precision=highest_precision) + jnp.einsum('hvt,hkt->hvk', imaginary_source_rows, real_block_piece, precision=highest_precision)
        return (real_totals + real_portion, imaginary_totals + imaginary_portion)
    zeros_start = jnp.zeros((NF, NS, NR), jnp.float32)
    real_totals, imaginary_totals = lax.fori_loop(0, block_count, add_block, (zeros_start, zeros_start))
    frequency_bins = jnp.arange(NF, dtype=jnp.int32)
    samples = jnp.arange(NT, dtype=jnp.int32)
    phases = (K0 + frequency_bins)[:, None] * samples[None, :] % NT
    angles = 2.0 * math.pi / NT * phases.astype(jnp.float32)
    weight = amplitude * math.sqrt(2.0 / NF)
    cosine_table = weight * jnp.cos(angles)
    sine_table = -weight * jnp.sin(angles)
    return jnp.einsum('mwb,mx->wbx', real_totals, cosine_table, precision=highest_precision) + jnp.einsum('mwb,mx->wbx', imaginary_totals, sine_table, precision=highest_precision)


def draw_recorded(key, part):
    multiples = predicted_traces(key)
    noise_key, scale_key = jax.random.split(jax.random.fold_in(key, 29))
    taps_key, gain_key = jax.random.split(jax.random.fold_in(key, 31))
    half_taps = (TAPS - 1) // 2
    true_taps = 0.08 * jax.random.normal(taps_key, (NS // WC, NR // WC, TAPS), jnp.float32)
    window_gain = jnp.exp(jax.random.uniform(gain_key, (NS // WC, NR // WC, 1), jnp.float32, math.log(0.5), math.log(2.0)))
    true_taps = true_taps * window_gain
    convolved = jnp.zeros((NS, NR, NT), jnp.float32)
    for tap_number in range(TAPS):
        shifted = jnp.roll(multiples, tap_number - half_taps, axis=2)
        tap_grid = jnp.repeat(jnp.repeat(true_taps[:, :, tap_number], WC, axis=0), WC, axis=1)
        convolved = convolved + tap_grid[:, :, None] * shifted
    noise = jax.random.truncated_normal(noise_key, -3.0, 3.0, (NS, NR, NT), jnp.float32)
    spread = jnp.exp(jax.random.uniform(scale_key, (NS, NR, 1), jnp.float32, 0.0, math.log(10.0))) / 4.0
    total = jnp.clip(convolved + noise * spread, -10.0, 10.0)
    tiles = total.reshape(ST, TS, 4 * FB, TR, NT)
    tiles = jnp.transpose(tiles, (0, 2, 1, 3, 4)).reshape(4 * ST * FB, TS, TR, NT)
    tiles = jnp.roll(tiles, -2 * FB, axis=0).reshape(4 * ST, FB, TS, TR, NT)
    return tiles.astype(jnp.bfloat16)


def block_levels(key, extent, cuts, low, high):
    factor_of = 1.0
    for dim, parts in cuts:
        draws = jax.random.uniform(jax.random.fold_in(jax.random.fold_in(key, 6), dim), (parts,), jnp.float32, low / len(cuts), high / len(cuts))
        factor_of = factor_of * jnp.repeat(jnp.exp(draws), extent[dim] // parts).reshape((-1,) + (1,) * (len(extent) - 1 - dim))
    return factor_of


def centred(stream_key, extent, deviation, bound, pieces=(), held_as=jnp.bfloat16):
    array = deviation * jax.random.normal(stream_key, extent, jnp.float32)
    if pieces:
        array = array * block_levels(stream_key, extent, pieces, -0.22, 0.18)
    return jnp.clip(array, -bound, bound).astype(held_as)


def setup_inputs(seed: int = 0, part: int = 0) -> dict:
    arg_keys = jax.random.split(jax.random.key(seed), 4)
    part_keys = jax.random.split(jax.random.fold_in(arg_keys[3], part), 4)
    return {
        "spectra": draw_spectra(jax.random.fold_in(jax.random.fold_in(arg_keys[3], part), 71), part),
        "recorded": draw_recorded(jax.random.fold_in(jax.random.fold_in(arg_keys[3], part), 71), part),
        "initial_filters": centred(part_keys[2], (N_REFL, N_FREQ, TS // WC, TR // WC, TAPS), 0.15, 0.6, ((0, 8), (1, 2)), jnp.float32),
    }


EXACT_PRECISION = lax.Precision.HIGHEST

def time_table():
    frequency_bins = jnp.arange(NF, dtype=jnp.int32)
    samples = jnp.arange(NT, dtype=jnp.int32)
    phases = (K0 + frequency_bins)[:, None] * samples[None, :] % NT
    angles = 2.0 * math.pi / NT * phases.astype(jnp.float32)
    weight = math.sqrt(2.0 / NF)
    return jnp.stack([weight * jnp.cos(angles), -weight * jnp.sin(angles)], axis=1).astype(jnp.bfloat16)

def lag_sums(matrix):
    length = matrix.shape[-1]
    leading = matrix.shape[:-2]
    doubled = jnp.concatenate([matrix, matrix], axis=-1).reshape(leading + (2 * length * length,))
    padded = jnp.concatenate([doubled, jnp.zeros(leading + (length,), matrix.dtype)], axis=-1)
    skewed = padded.reshape(leading + (length, 2 * length + 1))
    return lax.optimization_barrier(jnp.sum(skewed, axis=-2))[..., :length]

def solve_filters(gram_sums, cross_sums, initial):
    length = gram_sums.shape[-1]
    half_taps = (TAPS - 1) // 2
    lag_gram = lag_sums(gram_sums)[..., :TAPS]
    lag_cross = lag_sums(cross_sums)
    target = jnp.concatenate([jnp.flip(lag_cross[..., :half_taps + 1], -1), jnp.flip(lag_cross[..., length - half_taps:], -1)], -1)
    row_bound = lag_gram[..., 0] + 2.0 * lax.optimization_barrier(jnp.sum(jnp.abs(lag_gram[..., 1:]), -1))
    step_size = 0.5 / (row_bound + 1e-06)
    tap_index = jnp.arange(TAPS, dtype=jnp.int32)
    offset = jnp.abs(tap_index[:, None] - tap_index[None, :])
    select = (offset[:, :, None] == tap_index[None, None, :]).astype(jnp.float32)
    toeplitz = jnp.einsum('abk,...k->...ab', select, lag_gram, precision=EXACT_PRECISION)
    filters = initial
    for repeat in range(ITERS):
        applied = jnp.einsum('...ab,...b->...a', toeplitz, filters, precision=EXACT_PRECISION)
        filters = filters + step_size[..., None] * (target - applied)
    return filters

def conv_matrix(taps):
    half_taps = (TAPS - 1) // 2
    positions = jnp.arange(NT, dtype=jnp.int32)
    circular_shift = (positions[None, :] - positions[:, None]) % NT
    wanted = (jnp.arange(TAPS, dtype=jnp.int32) - half_taps) % NT
    select = (circular_shift[None] == wanted[:, None, None]).astype(jnp.float32)
    return jnp.einsum('kut,...k->...ut', select, taps.astype(jnp.float32), precision=EXACT_PRECISION).astype(jnp.bfloat16)

def to_grid(tiles):
    source_rows = N_REFL // 4
    columns = 4 * N_FREQ
    shape = tiles.shape
    flat = tiles.reshape((N_REFL * N_FREQ,) + shape[2:])
    flat = jnp.roll(flat, 2 * N_FREQ, axis=0)
    grouped = flat.reshape((source_rows, columns) + shape[2:])
    order = (0, 2, 1, 3) + tuple(range(4, grouped.ndim))
    moved = jnp.transpose(grouped, order)
    return moved.reshape((source_rows * shape[2], columns * shape[3]) + shape[4:])

def from_grid(grid, across, along):
    source_rows = N_REFL // 4
    columns = 4 * N_FREQ
    rest = grid.shape[2:]
    split = grid.reshape((source_rows, across, columns, along) + rest)
    order = (0, 2, 1, 3) + tuple(range(4, split.ndim))
    flat = jnp.transpose(split, order).reshape((N_REFL * N_FREQ, across, along) + rest)
    flat = jnp.roll(flat, -2 * N_FREQ, axis=0)
    return flat.reshape((N_REFL, N_FREQ, across, along) + rest)

def reference(spectra, recorded, initial_filters):
    block_width = XR // N_REFL
    amplitude = 1.0 / math.sqrt(2.0 * XR)

    def add_block(block_index, carry):
        real_totals, imaginary_totals = carry
        first_point = (block_index * block_width).astype(jnp.int32)
        block_piece = lax.dynamic_slice_in_dim(spectra, first_point, block_width, 3).astype(jnp.float32)
        real_full = block_piece[0]
        imaginary_full = block_piece[1]
        real_source_rows = real_full[:, :NS]
        imaginary_source_rows = imaginary_full[:, :NS]
        real_portion = jnp.einsum('hvt,hkt->hvk', real_source_rows, real_full) - jnp.einsum('hvt,hkt->hvk', imaginary_source_rows, imaginary_full)
        imaginary_portion = jnp.einsum('hvt,hkt->hvk', real_source_rows, imaginary_full) + jnp.einsum('hvt,hkt->hvk', imaginary_source_rows, real_full)
        rounded_real = lax.optimization_barrier((amplitude * real_portion).astype(jnp.bfloat16))
        rounded_imag = lax.optimization_barrier((amplitude * imaginary_portion).astype(jnp.bfloat16))
        return (real_totals + rounded_real.astype(jnp.float32), imaginary_totals + rounded_imag.astype(jnp.float32))
    zeros_start = jnp.zeros((NF, NS, NR), jnp.float32)
    real_totals, imaginary_totals = lax.fori_loop(0, N_REFL, add_block, (zeros_start, zeros_start))
    spectrum = jnp.stack([real_totals, imaginary_totals]).astype(jnp.bfloat16)
    multiples = jnp.einsum('afsr,fat->srt', spectrum.astype(jnp.float32), time_table().astype(jnp.float32)).astype(jnp.bfloat16)
    recorded_grid = to_grid(recorded)
    start_grid = to_grid(initial_filters)
    support_width = WC + 2 * WM
    pad_width = ((WM, WM), (WM, WM), (0, 0))
    padded_multiples = jnp.pad(multiples, pad_width)
    padded_recorded = jnp.pad(recorded_grid, pad_width)
    wins_rows = NS // WC
    wins_cols = NR // WC

    def one_window(window_index):
        row_index = window_index // wins_cols
        column_index = window_index % wins_cols
        row_start = (row_index * WC).astype(jnp.int32)
        column_start = (column_index * WC).astype(jnp.int32)
        zero_start = jnp.zeros((), jnp.int32)
        support_multiples = lax.dynamic_slice(padded_multiples, (row_start, column_start, zero_start), (support_width, support_width, NT)).reshape(support_width * support_width, NT)
        support_recorded = lax.dynamic_slice(padded_recorded, (row_start, column_start, zero_start), (support_width, support_width, NT)).reshape(support_width * support_width, NT)
        gram_sums = jnp.dot(support_multiples.T, support_multiples, preferred_element_type=jnp.float32)
        cross_sums = jnp.dot(support_recorded.T, support_multiples, preferred_element_type=jnp.float32)
        filters = solve_filters(gram_sums, cross_sums, start_grid[row_index, column_index])
        core_multiples = lax.dynamic_slice(padded_multiples, (row_start + WM, column_start + WM, zero_start), (WC, WC, NT)).reshape(WC * WC, NT)
        core_recorded = lax.dynamic_slice(padded_recorded, (row_start + WM, column_start + WM, zero_start), (WC, WC, NT)).reshape(WC * WC, NT)
        predicted = jnp.dot(core_multiples, conv_matrix(filters.astype(jnp.bfloat16)), preferred_element_type=jnp.float32)
        cleaned = (core_recorded.astype(jnp.float32) - predicted).astype(jnp.bfloat16).reshape(WC, WC, NT)
        return (filters, cleaned)
    filters_all, cleaned_all = lax.map(one_window, jnp.arange(wins_rows * wins_cols, dtype=jnp.int32))
    cleaned_grid = jnp.transpose(cleaned_all.reshape(wins_rows, wins_cols, WC, WC, NT), (0, 2, 1, 3, 4)).reshape(NS, NR, NT)
    primaries = from_grid(cleaned_grid, TS, TR)
    filters_out = from_grid(filters_all.reshape(wins_rows, wins_cols, TAPS), TS // WC, TR // WC)
    return (primaries, filters_out)
```

```python
import functools
import math

import jax
import jax.numpy as jnp
import ml_dtypes
import numpy as np
from jax import lax
from jax.experimental import pallas as pl
from jax.experimental.pallas import tpu as pltpu
from jax.sharding import PartitionSpec as P

NF = 16
K0 = 48
NT = 256
XR = 8192
WC = 32
WM = 4
TAPS = 33
ITERS = 3
HALF = (TAPS - 1) // 2
LAG = 2
ZLAG = 3
DEPTH = 3
EXACT = lax.Precision.HIGHEST


def angles_of(steps):
    bins = K0 + np.arange(NF)
    return 2.0 * math.pi / NT * ((bins[:, None] * steps[None, :]) % NT)


def time_rows():
    angles = angles_of(np.arange(NT))
    weight = math.sqrt(2.0 / NF)
    return np.concatenate([weight * np.cos(angles), -weight * np.sin(angles)], 0)


def filter_tables():
    tap_angles = angles_of(np.arange(TAPS) - HALF)
    basis = np.concatenate([np.cos(tap_angles), np.sin(tap_angles)], 0)
    lags = np.cos(angles_of(np.arange(TAPS))) * (NT / 2) * (2.0 / NF)
    lags = np.concatenate([lags, np.zeros_like(lags)], 0)
    return basis, basis @ basis.T, lags


def lane_selection(tr):
    lane = np.arange(2 * tr)
    receiver = lane % tr
    rows = np.zeros((3, 8, 2 * tr), np.float32)
    for kind, within in enumerate((lane >= 0, lane < tr, lane >= tr)):
        rows[kind, 0] = within & (receiver < WC + WM)
        rows[kind, 1] = within & (receiver >= tr - WC - WM)
        rows[kind, 2] = within & (receiver >= tr - WM)
        rows[kind, 5] = within & (receiver < WM)
    rows = rows.reshape(24, 2 * tr)
    return np.concatenate([rows, rows], 1)


def dot_nt(a, b, precision=None):
    return lax.dot_general(
        a, b, (((1,), (1,)), ((), ())), precision=precision,
        preferred_element_type=jnp.float32,
    )


def dot_nn(a, b, precision=None):
    return lax.dot_general(
        a, b, (((1,), (0,)), ((), ())), precision=precision,
        preferred_element_type=jnp.float32,
    )


def split(x):
    high = x.astype(jnp.bfloat16)
    low = (x - high.astype(jnp.float32)).astype(jnp.bfloat16)
    return jnp.concatenate([high, low], 1)


def kernel(
    n_refl, n_freq, sources,
    spectra_hbm, recorded_hbm, start_hbm, tables_hbm,
    shaped_ref, filters_ref, rec, table_ref,
    start_ref, tables, spec, part, yrecv, zsend, zrecv, csum, crecv, dat, xt, every, edge,
    stat, hrecv,
    spec_sem, rec_sem, start_sem, tables_sem, ysend_sem, yrecv_sem, zsend_sem, zrecv_sem,
    csend_sem, crecv_sem, hsend_sem, hrecv_sem,
):
    nf = spec.shape[0]
    ts, tr = rec.shape[0], rec.shape[1]
    half = ts // 2
    lanes = 2 * tr
    nz = n_refl // 2
    total = n_refl * n_freq
    columns = 4 * n_freq
    rows = total // columns
    amplitude = 1.0 / math.sqrt(2.0 * XR)
    refl = lax.axis_index("refl")
    core = lax.axis_index("freq")
    me = refl * n_freq + core
    z = refl // 2
    y = refl % 2
    partner = {"refl": z * 2 + (1 - y), "freq": core}
    twin = {"refl": refl, "freq": 1 - core}

    def device(linear):
        return {"refl": linear // n_freq, "freq": linear % n_freq}

    def spec_copy(f):
        return pltpu.make_async_copy(spectra_hbm.at[:, f], spec.at[f], spec_sem.at[f])

    side_copies = [
        pltpu.make_async_copy(recorded_hbm, rec, rec_sem),
        pltpu.make_async_copy(tables_hbm, tables, tables_sem),
        pltpu.make_async_copy(start_hbm, start_ref, start_sem),
    ]

    for f in range(DEPTH):
        spec_copy(f).start()

    barrier = pltpu.get_barrier_semaphore()

    directions = [(dp, dq) for dp in (-1, 0, 1) for dq in (-1, 0, 1) if dp or dq]
    offsets = sorted({(dp * columns + dq) % total for dp, dq in directions} - {0})
    met = [partner, twin]
    met += [{"refl": (z + dz) % nz * 2 + y, "freq": core} for dz in range(1, nz)]
    met += [device((me + offset) % total) for offset in offsets]
    for peer in met:
        pl.semaphore_signal(
            barrier, inc=1, device_id=peer, device_id_type=pl.DeviceIdType.MESH
        )

    lane = lax.broadcasted_iota(jnp.int32, (half, lanes), 1)
    low = lane < tr

    def y_copy(f):
        return pltpu.make_async_remote_copy(
            src_ref=part.at[1 - y, f], dst_ref=yrecv.at[f],
            send_sem=ysend_sem.at[f], recv_sem=yrecv_sem.at[f],
            device_id=partner, device_id_type=pl.DeviceIdType.MESH,
        )

    def z_copy(f, dz):
        to_z = (z + dz) % nz
        return pltpu.make_async_remote_copy(
            src_ref=zsend.at[f, to_z], dst_ref=zrecv.at[f, dz],
            send_sem=zsend_sem.at[f, dz], recv_sem=zrecv_sem.at[f, dz],
            device_id={"refl": to_z * 2 + y, "freq": core},
            device_id_type=pl.DeviceIdType.MESH,
        )

    def c_copy(f):
        return pltpu.make_async_remote_copy(
            src_ref=csum.at[f, 1 - core], dst_ref=crecv.at[f],
            send_sem=csend_sem.at[f], recv_sem=crecv_sem.at[f],
            device_id=twin, device_id_type=pl.DeviceIdType.MESH,
        )

    def products(f):
        real = spec[f, 0, :sources] * jnp.bfloat16(amplitude)
        imag = spec[f, 1, :sources] * jnp.bfloat16(amplitude)
        by_real = jnp.concatenate([real, imag], 0)
        by_imag = jnp.concatenate([-imag, real], 0)
        def one(turn, carry):
            parity = (1 - y) * (1 - turn) + y * turn
            spans = [
                pl.ds(pl.multiple_of((parity + 2 * g) * lanes, lanes), lanes)
                for g in range(2)
            ]
            terms = dot_nt(
                by_real, jnp.concatenate([spec[f, 0, span] for span in spans], 0)
            ) + dot_nt(
                by_imag, jnp.concatenate([spec[f, 1, span] for span in spans], 0)
            )
            for g in range(2):
                for p in range(n_refl // 4):
                    to_z = (4 * p + 2 * g - 2) % n_refl // 2
                    for c in range(2):
                        row = c * sources + p * ts
                        a = terms[row : row + half, g * lanes : (g + 1) * lanes]
                        b = terms[row + half : row + ts, g * lanes : (g + 1) * lanes]
                        turned = pltpu.roll(jnp.where(low, b, a), tr, 1)
                        part[parity, f, to_z, 0, c] = jnp.where(low, a, turned).astype(
                            jnp.bfloat16
                        )
                        part[parity, f, to_z, 1, c] = jnp.where(low, turned, b).astype(
                            jnp.bfloat16
                        )
            @pl.when((turn == 0) & (f == 0))
            def _():
                pl.semaphore_wait(barrier, len(met))

            @pl.when(turn == 0)
            def _():
                y_copy(f).start()

            return carry

        lax.fori_loop(0, 2, one, 0)

    def forward(f):
        y_copy(f).wait_recv()
        zsend[f] = (
            part[y, f].astype(jnp.float32) + yrecv[f].astype(jnp.float32)
        ).astype(jnp.bfloat16)
        for dz in range(1, nz):
            z_copy(f, dz).start()

    def z_arrival(f, dz):
        return pltpu.make_async_remote_copy(
            src_ref=zsend.at[f, z], dst_ref=zrecv.at[f, dz],
            send_sem=zsend_sem.at[f, dz], recv_sem=zrecv_sem.at[f, dz],
            device_id=partner, device_id_type=pl.DeviceIdType.MESH,
        )

    def gather(f):
        for dz in range(1, nz):
            z_arrival(f, dz).wait_recv()
        summed = zsend[f, z].astype(jnp.float32)
        for dz in range(1, nz):
            summed = summed + zrecv[f, dz].astype(jnp.float32)
        csum[f] = summed.astype(jnp.bfloat16)
        c_copy(f).start()

    def absorb(f):
        c_copy(f).wait_recv()
        source = lax.broadcasted_iota(jnp.int32, (half, lanes), 0)
        outer = (low & (source < WM)) | (~low & (source >= half - WM))
        for owner, block in ((core, csum.at[f, core]), (1 - core, crecv.at[f])):
            index = owner * nf + f
            xr = block[0].astype(jnp.float32)
            xi = block[1].astype(jnp.float32)
            d0 = dat[pl.ds(pl.multiple_of(index * half, half), half), :]
            d1 = dat[pl.ds(pl.multiple_of((NF + index) * half, half), half), :]
            sums = (xr * xr + xi * xi, xr * d0 + xi * d1, xi * d0 - xr * d1)
            for k in range(3):
                every[pl.ds(k * NF + index, 1), :] = jnp.sum(sums[k], 0, keepdims=True)
                edge[pl.ds(k * NF + index, 1), :] = jnp.sum(
                    jnp.where(outer, sums[k], 0.0), 0, keepdims=True
                )
            xt[pl.ds(index, half, stride=2 * NF), :] = xr
            xt[pl.ds(NF + index, half, stride=2 * NF), :] = xi

    def steady(f, carry):
        spec_copy(f).wait()

        @pl.when((f > 0) & (f + DEPTH - 1 < nf))
        def _():
            spec_copy(f + DEPTH - 1).start()

        products(f)

        @pl.when(f >= LAG)
        def _():
            forward(f - LAG)

        @pl.when(f >= LAG + ZLAG)
        def _():
            gather(f - LAG - ZLAG)

        return carry

    for copy in side_copies:
        copy.start()
    lax.fori_loop(0, nf, steady, 0)

    for copy in side_copies:
        copy.wait()
    table = tables[0 : 2 * NF].astype(jnp.bfloat16)
    basis = tables[2 * NF : 4 * NF, :TAPS]
    lags = tables[2 * NF : 4 * NF, lanes : lanes + TAPS]
    gram = tables[4 * NF : 6 * NF, : 2 * NF]
    sel = tables[6 * NF : 6 * NF + 24].astype(jnp.bfloat16)
    table_ref[...] = table

    def project(s, carry):
        traces = jnp.concatenate([rec[s], rec[half + s]], 0)
        dat[pl.ds(s, 2 * NF, stride=half), :] = dot_nt(table, traces)
        return carry

    lax.fori_loop(0, half, project, 0, unroll=4)
    start = start_ref[...]
    u0 = dot_nt(start, basis, EXACT)

    def drain(f, carry):
        @pl.when(f < nf)
        def _():
            forward(f)

        gather(f - ZLAG)
        return carry

    lax.fori_loop(nf - LAG, nf + ZLAG, drain, 0)

    def absorb_step(f, carry):
        absorb(f)
        return carry

    lax.fori_loop(0, nf, absorb_step, 0)

    tall = jnp.concatenate([every[:NF], every[...]], 0)
    stat[0, :, : 4 * NF] = dot_nt(sel[:8], split(tall))
    tall = jnp.concatenate([edge[:NF], edge[...]], 0)
    edges = dot_nt(sel[8:], split(tall))
    stat[1, :, : 4 * NF] = edges[:8]
    stat[2, :, : 4 * NF] = edges[8:]

    place = (me + 2 * n_freq) % total
    p, q = place // columns, place % columns

    def halo_copy(j):
        slot = offsets.index((total - offsets[j]) % total)
        if offsets[j] in (1, total - 1):
            kind = 0
        else:
            kind = 1 + jnp.where((place + offsets[j]) % total // columns > p, 1, 0)
        return pltpu.make_async_remote_copy(
            src_ref=stat.at[kind], dst_ref=hrecv.at[slot],
            send_sem=hsend_sem.at[j], recv_sem=hrecv_sem.at[slot],
            device_id=device((me + offsets[j]) % total),
            device_id_type=pl.DeviceIdType.MESH,
        )

    copies = [halo_copy(j) for j in range(len(offsets))]
    for copy in copies[1:-1] + [copies[0], copies[-1]]:
        copy.start()

    def settle(f, carry):
        y_copy(f).wait_send()
        for dz in range(1, nz):
            z_copy(f, dz).wait_send()
        c_copy(f).wait_send()
        return carry

    lax.fori_loop(0, nf, settle, 0)
    for copy in copies:
        copy.wait_recv()

    windows = stat[0, 0:2, : 4 * NF]
    for dp, dq in directions:
        slot = offsets.index((dp * columns + dq) % total)
        first = {-1: 2, 0: 0, 1: 4}[dq]
        inside = (p + dp >= 0) & (p + dp < rows) & (q + dq >= 0) & (q + dq < columns)
        windows = windows + jnp.where(
            inside, hrecv[slot, first : first + 2, : 4 * NF], 0.0
        )

    power = windows[:, : 2 * NF]
    cross = windows[:, 2 * NF : 4 * NF]
    lag_gram = dot_nn(power, lags, EXACT)
    tap = lax.broadcasted_iota(jnp.int32, lag_gram.shape, 1)
    bound = jnp.sum(jnp.where(tap == 0, lag_gram, 2.0 * jnp.abs(lag_gram)), 1, keepdims=True)
    step = 0.5 / (bound + 1e-06)
    weight = power * ((NT / 2) * (2.0 / NF))
    v = step * (cross - weight * u0)
    for _ in range(ITERS - 1):
        u = u0 + dot_nn(v, gram, EXACT)
        v = v + step * (cross - weight * u)
    filters = start + dot_nn(v, basis, EXACT)
    filters_ref[...] = filters
    taps = filters.astype(jnp.bfloat16).astype(jnp.float32)
    response = dot_nt(basis, taps, EXACT)
    window_of = lax.broadcasted_iota(jnp.int32, (NF, lanes), 1) % tr < WC
    hc = jnp.where(window_of, response[:NF, 0:1], response[:NF, 1:2])
    hs = jnp.where(window_of, response[NF:, 0:1], response[NF:, 1:2])

    for s in range(half):
        xr = xt[2 * NF * s : 2 * NF * s + NF]
        xi = xt[2 * NF * s + NF : 2 * NF * (s + 1)]
        shaped = jnp.concatenate([xr * hc + xi * hs, xi * hc - xr * hs], 0)
        shaped_ref[s] = shaped.astype(jnp.bfloat16)

    for copy in copies:
        copy.wait_send()


def subtract(
    shaped_ref, filters_ref, rec, table_ref, primaries_hbm, filters_hbm,
    outv, out_sem, filters_sem,
):
    half, tr = shaped_ref.shape[0], rec.shape[1]
    group = half // out_sem.shape[0]
    filters_copy = pltpu.make_async_copy(filters_ref, filters_hbm, filters_sem)
    filters_copy.start()
    copies = []
    for s in range(half):
        predicted = lax.dot_general(
            shaped_ref[s], table_ref[...], (((0,), (0,)), ((), ())),
            preferred_element_type=jnp.float32,
        )
        outv[s] = (rec[s].astype(jnp.float32) - predicted[:tr]).astype(jnp.bfloat16)
        outv[half + s] = (
            rec[half + s].astype(jnp.float32) - predicted[tr:]
        ).astype(jnp.bfloat16)
        if s % group == group - 1:
            for h in range(2):
                span = pl.ds(h * half + s - group + 1, group)
                copy = pltpu.make_async_copy(
                    outv.at[span], primaries_hbm.at[span], out_sem.at[s // group, h]
                )
                copy.start()
                copies.append(copy)
    for copy in copies + [filters_copy]:
        copy.wait()


def body(mesh_shape, spectra, recorded, initial_filters):
    n_refl, n_freq = mesh_shape["refl"], mesh_shape["freq"]
    nf, receivers, points = spectra.shape[1:]
    ts, tr, samples = recorded.shape[2:]
    sources = ts * (n_refl // 4)
    nz = n_refl // 2
    half, lanes = ts // 2, 2 * tr
    total, columns = n_refl * n_freq, 4 * n_freq
    n_halo = len(
        {(dp * columns + dq) % total for dp in (-1, 0, 1) for dq in (-1, 0, 1)} - {0}
    )
    basis, gram, lags = filter_tables()
    vmem = pl.BlockSpec(memory_space=pltpu.VMEM)
    hbm = pl.BlockSpec(memory_space=pltpu.HBM)
    tables = np.zeros((6 * NF + 24, max(samples, 2 * lanes)), np.float32)
    tables[: 2 * NF, :samples] = time_rows().astype(ml_dtypes.bfloat16).astype(np.float32)
    tables[2 * NF : 4 * NF, :TAPS] = basis
    tables[2 * NF : 4 * NF, lanes : lanes + TAPS] = lags
    tables[4 * NF : 6 * NF, : 2 * NF] = gram
    tables[6 * NF :] = lane_selection(tr)
    bf16, f32 = jnp.bfloat16, jnp.float32
    staged = pl.pallas_call(
        functools.partial(kernel, n_refl, n_freq, sources),
        out_shape=(
            jax.ShapeDtypeStruct((half, 2 * NF, lanes), bf16),
            jax.ShapeDtypeStruct((2, TAPS), f32),
            jax.ShapeDtypeStruct((ts, tr, samples), bf16),
            jax.ShapeDtypeStruct((2 * NF, samples), bf16),
        ),
        in_specs=[hbm] * 4,
        out_specs=(vmem,) * 4,
        scratch_shapes=[
            pltpu.VMEM((2, TAPS), f32),
            pltpu.VMEM(tables.shape, f32),
            pltpu.VMEM((nf, 2, receivers, points), bf16),
            pltpu.VMEM((2, nf, nz, n_freq, 2, half, lanes), bf16),
            pltpu.VMEM((nf, nz, n_freq, 2, half, lanes), bf16),
            pltpu.VMEM((nf, nz, n_freq, 2, half, lanes), bf16),
            pltpu.VMEM((nf, nz, n_freq, 2, half, lanes), bf16),
            pltpu.VMEM((nf, n_freq, 2, half, lanes), bf16),
            pltpu.VMEM((nf, 2, half, lanes), bf16),
            pltpu.VMEM((2 * NF * half, lanes), f32),
            pltpu.VMEM((half * 2 * NF, lanes), f32),
            pltpu.VMEM((3 * NF, lanes), f32),
            pltpu.VMEM((3 * NF, lanes), f32),
            pltpu.VMEM((3, 8, lanes), f32),
            pltpu.VMEM((n_halo, 8, lanes), f32),
            pltpu.SemaphoreType.DMA((nf,)),
            pltpu.SemaphoreType.DMA,
            pltpu.SemaphoreType.DMA,
            pltpu.SemaphoreType.DMA,
            pltpu.SemaphoreType.DMA((nf,)),
            pltpu.SemaphoreType.DMA((nf,)),
            pltpu.SemaphoreType.DMA((nf, nz)),
            pltpu.SemaphoreType.DMA((nf, nz)),
            pltpu.SemaphoreType.DMA((nf,)),
            pltpu.SemaphoreType.DMA((nf,)),
            pltpu.SemaphoreType.DMA((n_halo,)),
            pltpu.SemaphoreType.DMA((n_halo,)),
        ],
        compiler_params=pltpu.CompilerParams(
            collective_id=0, has_side_effects=True, vmem_limit_bytes=62 * 1024 * 1024
        ),
    )(
        spectra,
        recorded.reshape(ts, tr, samples),
        initial_filters.reshape(2, TAPS),
        jnp.asarray(tables),
    )
    primaries, filters = pl.pallas_call(
        subtract,
        out_shape=(
            jax.ShapeDtypeStruct((ts, tr, samples), bf16),
            jax.ShapeDtypeStruct((2, TAPS), f32),
        ),
        in_specs=[vmem] * 4,
        out_specs=(hbm, hbm),
        scratch_shapes=[
            pltpu.VMEM((ts, tr, samples), bf16),
            pltpu.SemaphoreType.DMA((4, 2)),
            pltpu.SemaphoreType.DMA,
        ],
        compiler_params=pltpu.CompilerParams(vmem_limit_bytes=62 * 1024 * 1024),
    )(*staged)
    return (
        primaries.reshape(recorded.shape),
        filters.reshape(initial_filters.shape),
    )


def solution(mesh):
    placed = (
        P(None, "freq", "groups", "refl"),
        P("refl", "freq", "groups", None, None),
        P("refl", "freq", "groups", None, None),
    )
    return jax.shard_map(
        functools.partial(body, dict(mesh.shape)),
        mesh=mesh,
        in_specs=placed,
        out_specs=(
            P("refl", "freq", "groups", None, None),
            P("refl", "freq", "groups", None, None),
        ),
        check_vma=False,
    )
```

```python
import functools
import math

import jax
import jax.numpy as jnp
import ml_dtypes
import numpy as np
from jax import lax
from jax.experimental import pallas as pl
from jax.experimental.pallas import tpu as pltpu
from jax.sharding import PartitionSpec as P

NF = 16
K0 = 48
NT = 256
XR = 8192
WC = 32
WM = 4
TAPS = 33
ITERS = 3
HALF = (TAPS - 1) // 2
LAG = 2
ZLAG = 3
DEPTH = 3
EXACT = lax.Precision.HIGHEST


def angles_of(steps):
    bins = K0 + np.arange(NF)
    return 2.0 * math.pi / NT * ((bins[:, None] * steps[None, :]) % NT)


def time_rows():
    angles = angles_of(np.arange(NT))
    weight = math.sqrt(2.0 / NF)
    return np.concatenate([weight * np.cos(angles), -weight * np.sin(angles)], 0)


def filter_tables():
    tap_angles = angles_of(np.arange(TAPS) - HALF)
    basis = np.concatenate([np.cos(tap_angles), np.sin(tap_angles)], 0)
    lags = np.cos(angles_of(np.arange(TAPS))) * (NT / 2) * (2.0 / NF)
    lags = np.concatenate([lags, np.zeros_like(lags)], 0)
    return basis, basis @ basis.T, lags


def lane_selection(tr):
    lane = np.arange(2 * tr)
    receiver = lane % tr
    rows = np.zeros((3, 8, 2 * tr), np.float32)
    for kind, within in enumerate((lane >= 0, lane < tr, lane >= tr)):
        rows[kind, 0] = within & (receiver < WC + WM)
        rows[kind, 1] = within & (receiver >= tr - WC - WM)
        rows[kind, 2] = within & (receiver >= tr - WM)
        rows[kind, 5] = within & (receiver < WM)
    rows = rows.reshape(24, 2 * tr)
    return np.concatenate([rows, rows], 1)


def dot_nt(a, b, precision=None):
    return lax.dot_general(
        a, b, (((1,), (1,)), ((), ())), precision=precision,
        preferred_element_type=jnp.float32,
    )


def dot_nn(a, b, precision=None):
    return lax.dot_general(
        a, b, (((1,), (0,)), ((), ())), precision=precision,
        preferred_element_type=jnp.float32,
    )


def split(x):
    high = x.astype(jnp.bfloat16)
    low = (x - high.astype(jnp.float32)).astype(jnp.bfloat16)
    return jnp.concatenate([high, low], 1)


def kernel(
    n_refl, n_freq, sources,
    spectra_hbm, recorded_hbm, start_hbm, tables_hbm,
    shaped_ref, filters_ref, rec, table_ref,
    start_ref, tables, spec, part, yrecv, trecv, zsend, zrecv, csum, dat, xt, every, edge,
    stat, hrecv,
    spec_sem, rec_sem, start_sem, tables_sem, ysend_sem, yrecv_sem, zsend_sem, zrecv_sem,
    tsend_sem, trecv_sem, hsend_sem, hrecv_sem,
):
    nf = spec.shape[0]
    ts, tr = rec.shape[0], rec.shape[1]
    half = ts // 2
    lanes = 2 * tr
    nz = n_refl // 2
    total = n_refl * n_freq
    columns = 4 * n_freq
    rows = total // columns
    amplitude = 1.0 / math.sqrt(2.0 * XR)
    refl = lax.axis_index("refl")
    core = lax.axis_index("freq")
    me = refl * n_freq + core
    z = refl // 2
    y = refl % 2
    partner = {"refl": z * 2 + (1 - y), "freq": core}
    twin = {"refl": refl, "freq": 1 - core}

    def device(linear):
        return {"refl": linear // n_freq, "freq": linear % n_freq}

    def spec_copy(f):
        return pltpu.make_async_copy(spectra_hbm.at[:, f], spec.at[f], spec_sem.at[f])

    side_copies = [
        pltpu.make_async_copy(recorded_hbm, rec, rec_sem),
        pltpu.make_async_copy(tables_hbm, tables, tables_sem),
        pltpu.make_async_copy(start_hbm, start_ref, start_sem),
    ]

    for f in range(DEPTH):
        spec_copy(f).start()

    barrier = pltpu.get_barrier_semaphore()

    directions = [(dp, dq) for dp in (-1, 0, 1) for dq in (-1, 0, 1) if dp or dq]
    offsets = sorted({(dp * columns + dq) % total for dp, dq in directions} - {0})
    met = [partner, twin, {"refl": z * 2 + (1 - y), "freq": 1 - core}]
    met += [{"refl": (z + dz) % nz * 2 + y, "freq": core} for dz in range(1, nz)]
    met += [device((me + offset) % total) for offset in offsets]
    for peer in met:
        pl.semaphore_signal(
            barrier, inc=1, device_id=peer, device_id_type=pl.DeviceIdType.MESH
        )

    lane = lax.broadcasted_iota(jnp.int32, (half, lanes), 1)
    low = lane < tr

    def y_copy(f, other):
        to = (core + other) % 2
        return pltpu.make_async_remote_copy(
            src_ref=part.at[1 - y, to, f], dst_ref=yrecv.at[core, f],
            send_sem=ysend_sem.at[f, other], recv_sem=yrecv_sem.at[f, core],
            device_id={"refl": z * 2 + (1 - y), "freq": to},
            device_id_type=pl.DeviceIdType.MESH,
        )

    def y_arrival(f, sender):
        return pltpu.make_async_remote_copy(
            src_ref=part.at[1 - y, core, f], dst_ref=yrecv.at[sender, f],
            send_sem=ysend_sem.at[f, 0], recv_sem=yrecv_sem.at[f, sender],
            device_id=partner, device_id_type=pl.DeviceIdType.MESH,
        )

    def t_copy(f):
        return pltpu.make_async_remote_copy(
            src_ref=part.at[y, 1 - core, f], dst_ref=trecv.at[f],
            send_sem=tsend_sem.at[f], recv_sem=trecv_sem.at[f],
            device_id=twin, device_id_type=pl.DeviceIdType.MESH,
        )

    def z_copy(f, dz):
        to_z = (z + dz) % nz
        return pltpu.make_async_remote_copy(
            src_ref=zsend.at[f, to_z], dst_ref=zrecv.at[f, dz],
            send_sem=zsend_sem.at[f, dz], recv_sem=zrecv_sem.at[f, dz],
            device_id={"refl": to_z * 2 + y, "freq": core},
            device_id_type=pl.DeviceIdType.MESH,
        )

    def products(f):
        real = spec[f, 0, :sources] * jnp.bfloat16(amplitude)
        imag = spec[f, 1, :sources] * jnp.bfloat16(amplitude)
        by_real = jnp.concatenate([real, imag], 0)
        by_imag = jnp.concatenate([-imag, real], 0)
        def one(turn, carry):
            parity = (1 - y) * (1 - turn) + y * turn
            spans = [
                pl.ds(pl.multiple_of((parity + 2 * g) * lanes, lanes), lanes)
                for g in range(2)
            ]
            terms = dot_nt(
                by_real, jnp.concatenate([spec[f, 0, span] for span in spans], 0)
            ) + dot_nt(
                by_imag, jnp.concatenate([spec[f, 1, span] for span in spans], 0)
            )
            for g in range(2):
                for p in range(n_refl // 4):
                    to_z = (4 * p + 2 * g - 2) % n_refl // 2
                    for c in range(2):
                        row = c * sources + p * ts
                        a = terms[row : row + half, g * lanes : (g + 1) * lanes]
                        b = terms[row + half : row + ts, g * lanes : (g + 1) * lanes]
                        turned = pltpu.roll(jnp.where(low, b, a), tr, 1)
                        part[parity, 0, f, to_z, c] = jnp.where(low, a, turned).astype(
                            jnp.bfloat16
                        )
                        part[parity, 1, f, to_z, c] = jnp.where(low, turned, b).astype(
                            jnp.bfloat16
                        )
            @pl.when((turn == 0) & (f == 0))
            def _():
                pl.semaphore_wait(barrier, len(met))

            @pl.when(turn == 0)
            def _():
                y_copy(f, 0).start()
                y_copy(f, 1).start()

            @pl.when(turn == 1)
            def _():
                t_copy(f).start()

            return carry

        lax.fori_loop(0, 2, one, 0)

    def forward(f):
        t_copy(f).wait_recv()
        for sender in range(n_freq):
            y_arrival(f, sender).wait_recv()
        for owner, block in ((core, part.at[y, core, f]), (1 - core, trecv.at[f])):
            zsend[f, :, owner] = (
                block[...].astype(jnp.float32) + yrecv[owner, f].astype(jnp.float32)
            ).astype(jnp.bfloat16)
        for dz in range(1, nz):
            z_copy(f, dz).start()

    def z_arrival(f, dz):
        return pltpu.make_async_remote_copy(
            src_ref=zsend.at[f, z], dst_ref=zrecv.at[f, dz],
            send_sem=zsend_sem.at[f, dz], recv_sem=zrecv_sem.at[f, dz],
            device_id=partner, device_id_type=pl.DeviceIdType.MESH,
        )

    def gather(f):
        for dz in range(1, nz):
            z_arrival(f, dz).wait_recv()
        summed = zsend[f, z].astype(jnp.float32)
        for dz in range(1, nz):
            summed = summed + zrecv[f, dz].astype(jnp.float32)
        csum[f] = summed.astype(jnp.bfloat16)

    def absorb(f):
        source = lax.broadcasted_iota(jnp.int32, (half, lanes), 0)
        outer = (low & (source < WM)) | (~low & (source >= half - WM))
        for owner in range(n_freq):
            block = csum[f, owner]
            index = owner * nf + f
            xr = block[0].astype(jnp.float32)
            xi = block[1].astype(jnp.float32)
            d0 = dat[pl.ds(pl.multiple_of(index * half, half), half), :]
            d1 = dat[pl.ds(pl.multiple_of((NF + index) * half, half), half), :]
            sums = (xr * xr + xi * xi, xr * d0 + xi * d1, xi * d0 - xr * d1)
            for k in range(3):
                every[pl.ds(k * NF + index, 1), :] = jnp.sum(sums[k], 0, keepdims=True)
                edge[pl.ds(k * NF + index, 1), :] = jnp.sum(
                    jnp.where(outer, sums[k], 0.0), 0, keepdims=True
                )
            xt[pl.ds(index, half, stride=2 * NF), :] = xr
            xt[pl.ds(NF + index, half, stride=2 * NF), :] = xi

    def steady(f, carry):
        spec_copy(f).wait()

        @pl.when((f > 0) & (f + DEPTH - 1 < nf))
        def _():
            spec_copy(f + DEPTH - 1).start()

        products(f)

        @pl.when(f >= LAG)
        def _():
            forward(f - LAG)

        @pl.when(f >= LAG + ZLAG)
        def _():
            gather(f - LAG - ZLAG)

        return carry

    for copy in side_copies:
        copy.start()
    lax.fori_loop(0, nf, steady, 0)

    for copy in side_copies:
        copy.wait()
    table = tables[0 : 2 * NF].astype(jnp.bfloat16)
    basis = tables[2 * NF : 4 * NF, :TAPS]
    lags = tables[2 * NF : 4 * NF, lanes : lanes + TAPS]
    gram = tables[4 * NF : 6 * NF, : 2 * NF]
    sel = tables[6 * NF : 6 * NF + 24].astype(jnp.bfloat16)
    table_ref[...] = table

    def project(s, carry):
        traces = jnp.concatenate([rec[s], rec[half + s]], 0)
        dat[pl.ds(s, 2 * NF, stride=half), :] = dot_nt(table, traces)
        return carry

    lax.fori_loop(0, half, project, 0, unroll=4)
    start = start_ref[...]
    u0 = dot_nt(start, basis, EXACT)

    def drain(f, carry):
        @pl.when(f < nf)
        def _():
            forward(f)

        gather(f - ZLAG)
        return carry

    lax.fori_loop(nf - LAG, nf + ZLAG, drain, 0)

    def absorb_step(f, carry):
        absorb(f)
        return carry

    lax.fori_loop(0, nf, absorb_step, 0)

    tall = jnp.concatenate([every[:NF], every[...]], 0)
    stat[0, :, : 4 * NF] = dot_nt(sel[:8], split(tall))
    tall = jnp.concatenate([edge[:NF], edge[...]], 0)
    edges = dot_nt(sel[8:], split(tall))
    stat[1, :, : 4 * NF] = edges[:8]
    stat[2, :, : 4 * NF] = edges[8:]

    place = (me + 2 * n_freq) % total
    p, q = place // columns, place % columns

    def halo_copy(j):
        slot = offsets.index((total - offsets[j]) % total)
        if offsets[j] in (1, total - 1):
            kind = 0
        else:
            kind = 1 + jnp.where((place + offsets[j]) % total // columns > p, 1, 0)
        return pltpu.make_async_remote_copy(
            src_ref=stat.at[kind], dst_ref=hrecv.at[slot],
            send_sem=hsend_sem.at[j], recv_sem=hrecv_sem.at[slot],
            device_id=device((me + offsets[j]) % total),
            device_id_type=pl.DeviceIdType.MESH,
        )

    copies = [halo_copy(j) for j in range(len(offsets))]
    for copy in copies[1:-1] + [copies[0], copies[-1]]:
        copy.start()

    def settle(f, carry):
        y_copy(f, 0).wait_send()
        y_copy(f, 1).wait_send()
        t_copy(f).wait_send()
        for dz in range(1, nz):
            z_copy(f, dz).wait_send()
        return carry

    lax.fori_loop(0, nf, settle, 0)
    for copy in copies:
        copy.wait_recv()

    windows = stat[0, 0:2, : 4 * NF]
    for dp, dq in directions:
        slot = offsets.index((dp * columns + dq) % total)
        first = {-1: 2, 0: 0, 1: 4}[dq]
        inside = (p + dp >= 0) & (p + dp < rows) & (q + dq >= 0) & (q + dq < columns)
        windows = windows + jnp.where(
            inside, hrecv[slot, first : first + 2, : 4 * NF], 0.0
        )

    power = windows[:, : 2 * NF]
    cross = windows[:, 2 * NF : 4 * NF]
    lag_gram = dot_nn(power, lags, EXACT)
    tap = lax.broadcasted_iota(jnp.int32, lag_gram.shape, 1)
    bound = jnp.sum(jnp.where(tap == 0, lag_gram, 2.0 * jnp.abs(lag_gram)), 1, keepdims=True)
    step = 0.5 / (bound + 1e-06)
    weight = power * ((NT / 2) * (2.0 / NF))
    v = step * (cross - weight * u0)
    for _ in range(ITERS - 1):
        u = u0 + dot_nn(v, gram, EXACT)
        v = v + step * (cross - weight * u)
    filters = start + dot_nn(v, basis, EXACT)
    filters_ref[...] = filters
    taps = filters.astype(jnp.bfloat16).astype(jnp.float32)
    response = dot_nt(basis, taps, EXACT)
    window_of = lax.broadcasted_iota(jnp.int32, (NF, lanes), 1) % tr < WC
    hc = jnp.where(window_of, response[:NF, 0:1], response[:NF, 1:2])
    hs = jnp.where(window_of, response[NF:, 0:1], response[NF:, 1:2])

    for s in range(half):
        xr = xt[2 * NF * s : 2 * NF * s + NF]
        xi = xt[2 * NF * s + NF : 2 * NF * (s + 1)]
        shaped = jnp.concatenate([xr * hc + xi * hs, xi * hc - xr * hs], 0)
        shaped_ref[s] = shaped.astype(jnp.bfloat16)

    for copy in copies:
        copy.wait_send()


def subtract(
    shaped_ref, filters_ref, rec, table_ref, primaries_hbm, filters_hbm,
    outv, out_sem, filters_sem,
):
    half, tr = shaped_ref.shape[0], rec.shape[1]
    group = half // out_sem.shape[0]
    filters_copy = pltpu.make_async_copy(filters_ref, filters_hbm, filters_sem)
    filters_copy.start()
    copies = []
    for s in range(half):
        predicted = lax.dot_general(
            shaped_ref[s], table_ref[...], (((0,), (0,)), ((), ())),
            preferred_element_type=jnp.float32,
        )
        outv[s] = (rec[s].astype(jnp.float32) - predicted[:tr]).astype(jnp.bfloat16)
        outv[half + s] = (
            rec[half + s].astype(jnp.float32) - predicted[tr:]
        ).astype(jnp.bfloat16)
        if s % group == group - 1:
            for h in range(2):
                span = pl.ds(h * half + s - group + 1, group)
                copy = pltpu.make_async_copy(
                    outv.at[span], primaries_hbm.at[span], out_sem.at[s // group, h]
                )
                copy.start()
                copies.append(copy)
    for copy in copies + [filters_copy]:
        copy.wait()


def body(mesh_shape, spectra, recorded, initial_filters):
    n_refl, n_freq = mesh_shape["refl"], mesh_shape["freq"]
    nf, receivers, points = spectra.shape[1:]
    ts, tr, samples = recorded.shape[2:]
    sources = ts * (n_refl // 4)
    nz = n_refl // 2
    half, lanes = ts // 2, 2 * tr
    total, columns = n_refl * n_freq, 4 * n_freq
    n_halo = len(
        {(dp * columns + dq) % total for dp in (-1, 0, 1) for dq in (-1, 0, 1)} - {0}
    )
    basis, gram, lags = filter_tables()
    vmem = pl.BlockSpec(memory_space=pltpu.VMEM)
    hbm = pl.BlockSpec(memory_space=pltpu.HBM)
    tables = np.zeros((6 * NF + 24, max(samples, 2 * lanes)), np.float32)
    tables[: 2 * NF, :samples] = time_rows().astype(ml_dtypes.bfloat16).astype(np.float32)
    tables[2 * NF : 4 * NF, :TAPS] = basis
    tables[2 * NF : 4 * NF, lanes : lanes + TAPS] = lags
    tables[4 * NF : 6 * NF, : 2 * NF] = gram
    tables[6 * NF :] = lane_selection(tr)
    bf16, f32 = jnp.bfloat16, jnp.float32
    staged = pl.pallas_call(
        functools.partial(kernel, n_refl, n_freq, sources),
        out_shape=(
            jax.ShapeDtypeStruct((half, 2 * NF, lanes), bf16),
            jax.ShapeDtypeStruct((2, TAPS), f32),
            jax.ShapeDtypeStruct((ts, tr, samples), bf16),
            jax.ShapeDtypeStruct((2 * NF, samples), bf16),
        ),
        in_specs=[hbm] * 4,
        out_specs=(vmem,) * 4,
        scratch_shapes=[
            pltpu.VMEM((2, TAPS), f32),
            pltpu.VMEM(tables.shape, f32),
            pltpu.VMEM((nf, 2, receivers, points), bf16),
            pltpu.VMEM((2, n_freq, nf, nz, 2, half, lanes), bf16),
            pltpu.VMEM((n_freq, nf, nz, 2, half, lanes), bf16),
            pltpu.VMEM((nf, nz, 2, half, lanes), bf16),
            pltpu.VMEM((nf, nz, n_freq, 2, half, lanes), bf16),
            pltpu.VMEM((nf, nz, n_freq, 2, half, lanes), bf16),
            pltpu.VMEM((nf, n_freq, 2, half, lanes), bf16),
            pltpu.VMEM((2 * NF * half, lanes), f32),
            pltpu.VMEM((half * 2 * NF, lanes), f32),
            pltpu.VMEM((3 * NF, lanes), f32),
            pltpu.VMEM((3 * NF, lanes), f32),
            pltpu.VMEM((3, 8, lanes), f32),
            pltpu.VMEM((n_halo, 8, lanes), f32),
            pltpu.SemaphoreType.DMA((nf,)),
            pltpu.SemaphoreType.DMA,
            pltpu.SemaphoreType.DMA,
            pltpu.SemaphoreType.DMA,
            pltpu.SemaphoreType.DMA((nf, n_freq)),
            pltpu.SemaphoreType.DMA((nf, n_freq)),
            pltpu.SemaphoreType.DMA((nf, nz)),
            pltpu.SemaphoreType.DMA((nf, nz)),
            pltpu.SemaphoreType.DMA((nf,)),
            pltpu.SemaphoreType.DMA((nf,)),
            pltpu.SemaphoreType.DMA((n_halo,)),
            pltpu.SemaphoreType.DMA((n_halo,)),
        ],
        compiler_params=pltpu.CompilerParams(
            collective_id=0, has_side_effects=True, vmem_limit_bytes=40 * 1024 * 1024
        ),
    )(
        *[
            pltpu.with_memory_space_constraint(x, pltpu.HBM)
            for x in (
                spectra,
                recorded.reshape(ts, tr, samples),
                initial_filters.reshape(2, TAPS),
                jnp.asarray(tables),
            )
        ]
    )
    primaries, filters = pl.pallas_call(
        subtract,
        out_shape=(
            jax.ShapeDtypeStruct((ts, tr, samples), bf16),
            jax.ShapeDtypeStruct((2, TAPS), f32),
        ),
        in_specs=[vmem] * 4,
        out_specs=(hbm, hbm),
        scratch_shapes=[
            pltpu.VMEM((ts, tr, samples), bf16),
            pltpu.SemaphoreType.DMA((4, 2)),
            pltpu.SemaphoreType.DMA,
        ],
        compiler_params=pltpu.CompilerParams(vmem_limit_bytes=40 * 1024 * 1024),
    )(*staged)
    return (
        primaries.reshape(recorded.shape),
        filters.reshape(initial_filters.shape),
    )


def solution(mesh):
    placed = (
        P(None, "freq", "groups", "refl"),
        P("refl", "freq", "groups", None, None),
        P("refl", "freq", "groups", None, None),
    )
    return jax.shard_map(
        functools.partial(body, dict(mesh.shape)),
        mesh=mesh,
        in_specs=placed,
        out_specs=(
            P("refl", "freq", "groups", None, None),
            P("refl", "freq", "groups", None, None),
        ),
        check_vma=False,
    )
```

```python
import functools
import math

import jax
import jax.numpy as jnp
import ml_dtypes
import numpy as np
from jax import lax
from jax.experimental import pallas as pl
from jax.experimental.pallas import tpu as pltpu
from jax.sharding import PartitionSpec as P

NF = 16
K0 = 48
NT = 256
XR = 8192
WC = 32
WM = 4
TAPS = 33
HALF = (TAPS - 1) // 2
LAG = 2
ZLAG = 3
DEPTH = 3
HEAD = 7
EXACT = lax.Precision.HIGHEST


def angles_of(steps):
    bins = K0 + np.arange(NF)
    return 2.0 * math.pi / NT * ((bins[:, None] * steps[None, :]) % NT)


def time_rows():
    angles = angles_of(np.arange(NT))
    weight = math.sqrt(2.0 / NF)
    return np.concatenate([weight * np.cos(angles), -weight * np.sin(angles)], 0)


def filter_tables():
    tap_angles = angles_of(np.arange(TAPS) - HALF)
    basis = np.concatenate([np.cos(tap_angles), np.sin(tap_angles)], 0)
    lags = np.cos(angles_of(np.arange(TAPS))) * (NT / 2) * (2.0 / NF)
    lags = np.concatenate([lags, np.zeros_like(lags)], 0)
    return basis, basis @ basis.T, lags


def lane_selection(tr):
    lane = np.arange(2 * tr)
    receiver = lane % tr
    rows = np.zeros((3, 8, 2 * tr), np.float32)
    for kind, within in enumerate((lane >= 0, lane < tr, lane >= tr)):
        rows[kind, 0] = within & (receiver < WC + WM)
        rows[kind, 1] = within & (receiver >= tr - WC - WM)
        rows[kind, 2] = within & (receiver >= tr - WM)
        rows[kind, 5] = within & (receiver < WM)
    rows = rows.reshape(24, 2 * tr)
    return np.concatenate([rows, rows], 1)


def dot_nt(a, b, precision=None):
    return lax.dot_general(
        a, b, (((1,), (1,)), ((), ())), precision=precision,
        preferred_element_type=jnp.float32,
    )


def dot_nn(a, b, precision=None):
    return lax.dot_general(
        a, b, (((1,), (0,)), ((), ())), precision=precision,
        preferred_element_type=jnp.float32,
    )


def split(x):
    high = x.astype(jnp.bfloat16)
    low = (x - high.astype(jnp.float32)).astype(jnp.bfloat16)
    return jnp.concatenate([high, low], 1)


def halves(x):
    high = x.astype(jnp.bfloat16)
    return high, (x - high.astype(jnp.float32)).astype(jnp.bfloat16)


def dot_halves(x, table):
    high, low = halves(x)
    return dot_nn(high, table[0]) + (dot_nn(low, table[0]) + dot_nn(high, table[1]))


def kernel(
    n_refl, n_freq, sources,
    spectra_hbm, recorded_hbm, start_hbm, tables_hbm,
    shaped_ref, filters_ref, rec, table_ref,
    start_ref, tables, spec, part, yrecv, trecv, zsend, zrecv, hrecv, hsum, hlast, csum, dat, xt, every, edge,
    stat, nrecv,
    spec_sem, rec_sem, start_sem, tables_sem, ysend_sem, yrecv_sem, zsend_sem, zrecv_sem,
    tsend_sem, trecv_sem, hsend_sem, hrecv_sem,
    lsend_sem, lrecv_sem, nsend_sem, nrecv_sem,
):
    nf = spec.shape[0]
    ts, tr = rec.shape[0], rec.shape[1]
    half = ts // 2
    lanes = 2 * tr
    nz = n_refl // 2
    total = n_refl * n_freq
    columns = 4 * n_freq
    rows = total // columns
    amplitude = 1.0 / math.sqrt(2.0 * XR)
    refl = lax.axis_index("refl")
    core = lax.axis_index("freq")
    me = refl * n_freq + core
    z = refl // 2
    y = refl % 2
    partner = {"refl": z * 2 + (1 - y), "freq": core}
    twin = {"refl": refl, "freq": 1 - core}

    def device(linear):
        return {"refl": linear // n_freq, "freq": linear % n_freq}

    def spec_copy(f):
        return pltpu.make_async_copy(spectra_hbm.at[:, f], spec.at[f], spec_sem.at[f])

    side_copies = [
        pltpu.make_async_copy(recorded_hbm, rec, rec_sem),
        pltpu.make_async_copy(tables_hbm, tables, tables_sem),
        pltpu.make_async_copy(start_hbm, start_ref, start_sem),
    ]

    for f in range(DEPTH):
        spec_copy(f).start()

    barrier = pltpu.get_barrier_semaphore()

    directions = [(dp, dq) for dp in (-1, 0, 1) for dq in (-1, 0, 1) if dp or dq]
    offsets = sorted({(dp * columns + dq) % total for dp, dq in directions} - {0})
    met = [partner, twin, {"refl": z * 2 + (1 - y), "freq": 1 - core}]
    met += [{"refl": (z + dz) % nz * 2 + y, "freq": core} for dz in range(1, nz)]
    met += [device((me + offset) % total) for offset in offsets]
    for peer in met:
        pl.semaphore_signal(
            barrier, inc=1, device_id=peer, device_id_type=pl.DeviceIdType.MESH
        )

    lane = lax.broadcasted_iota(jnp.int32, (half, lanes), 1)
    low = lane < tr

    def y_copy(f, other, turn):
        to = (core + other) % 2
        span = pl.ds(turn * (nz // 2), nz // 2)
        return pltpu.make_async_remote_copy(
            src_ref=part.at[1 - y, to, f, span], dst_ref=yrecv.at[core, f, span],
            send_sem=ysend_sem.at[f, turn, other], recv_sem=yrecv_sem.at[f, turn, core],
            device_id={"refl": z * 2 + (1 - y), "freq": to},
            device_id_type=pl.DeviceIdType.MESH,
        )

    def y_arrival(f, sender, turn):
        span = pl.ds(turn * (nz // 2), nz // 2)
        return pltpu.make_async_remote_copy(
            src_ref=part.at[1 - y, core, f, span], dst_ref=yrecv.at[sender, f, span],
            send_sem=ysend_sem.at[f, turn, 0], recv_sem=yrecv_sem.at[f, turn, sender],
            device_id=partner, device_id_type=pl.DeviceIdType.MESH,
        )

    def t_copy(f):
        return pltpu.make_async_remote_copy(
            src_ref=part.at[y, 1 - core, f], dst_ref=trecv.at[f],
            send_sem=tsend_sem.at[f], recv_sem=trecv_sem.at[f],
            device_id=twin, device_id_type=pl.DeviceIdType.MESH,
        )

    def z_copy(f, dz):
        to_z = (z + dz) % nz
        return pltpu.make_async_remote_copy(
            src_ref=zsend.at[f, to_z], dst_ref=zrecv.at[f, dz],
            send_sem=zsend_sem.at[f, dz], recv_sem=zrecv_sem.at[f, dz],
            device_id={"refl": to_z * 2 + y, "freq": core},
            device_id_type=pl.DeviceIdType.MESH,
        )

    def h_copy(turn, dz):
        to_z = (z + dz) % nz
        parity = (y + 1 - turn) % 2
        return pltpu.make_async_remote_copy(
            src_ref=part.at[parity, :, 0, to_z], dst_ref=hrecv.at[turn, dz],
            send_sem=hsend_sem.at[turn, dz], recv_sem=hrecv_sem.at[turn, dz],
            device_id={"refl": to_z * 2 + y, "freq": core},
            device_id_type=pl.DeviceIdType.MESH,
        )

    def l_copy(k):
        to = core if k == 0 else 1 - core
        return pltpu.make_async_remote_copy(
            src_ref=hsum.at[k // 2, to], dst_ref=hlast.at[k],
            send_sem=lsend_sem.at[k], recv_sem=lrecv_sem.at[k],
            device_id=(partner, met[2], twin)[k], device_id_type=pl.DeviceIdType.MESH,
        )

    def products(f):
        real = spec[f, 0, :sources] * jnp.bfloat16(amplitude)
        imag = spec[f, 1, :sources] * jnp.bfloat16(amplitude)
        by_real = jnp.concatenate([real, imag], 0)
        by_imag = jnp.concatenate([-imag, real], 0)
        def one(turn, carry):
            parity = (1 - y) * (1 - turn) + y * turn
            spans = [
                pl.ds(pl.multiple_of((parity + 2 * g) * lanes, lanes), lanes)
                for g in range(2)
            ]
            terms = dot_nt(
                by_real, jnp.concatenate([spec[f, 0, span] for span in spans], 0)
            ) + dot_nt(
                by_imag, jnp.concatenate([spec[f, 1, span] for span in spans], 0)
            )
            for g in range(2):
                for p in range(n_refl // 4):
                    to_z = (4 * p + 2 * g - 2) % n_refl // 2
                    for c in range(2):
                        row = c * sources + p * ts
                        a = terms[row : row + half, g * lanes : (g + 1) * lanes]
                        b = terms[row + half : row + ts, g * lanes : (g + 1) * lanes]
                        turned = pltpu.roll(jnp.where(low, b, a), tr, 1)
                        part[parity, 0, f, to_z, c] = jnp.where(low, a, turned).astype(
                            jnp.bfloat16
                        )
                        part[parity, 1, f, to_z, c] = jnp.where(low, turned, b).astype(
                            jnp.bfloat16
                        )
            @pl.when((turn == 0) & (f == 0))
            def _():
                pl.semaphore_wait(barrier, len(met))

            @pl.when(f == 0)
            def _():
                for dz in range(1, nz):
                    h_copy(turn, dz).start()

            @pl.when((turn == 0) & (f > 0))
            def _():
                for piece in range(2):
                    for other in range(n_freq):
                        y_copy(f, other, piece).start()

            @pl.when((turn == 1) & (f > 0))
            def _():
                t_copy(f).start()

            return carry

        lax.fori_loop(0, 2, one, 0)

    def forward(f):
        t_copy(f).wait_recv()
        for piece in range(2):
            for sender in range(n_freq):
                y_arrival(f, sender, piece).wait_recv()
            span = slice(piece * (nz // 2), (piece + 1) * (nz // 2))
            for owner, block in ((core, part.at[y, core, f]), (1 - core, trecv.at[f])):
                zsend[f, span, owner] = (
                    block[span].astype(jnp.float32) + yrecv[owner, f, span].astype(jnp.float32)
                ).astype(jnp.bfloat16)
            for to_z in range(piece * (nz // 2), (piece + 1) * (nz // 2)):
                @pl.when(z != to_z)
                def _():
                    z_copy(f, (to_z - z + nz) % nz).start()

    def z_arrival(f, dz):
        return pltpu.make_async_remote_copy(
            src_ref=zsend.at[f, z], dst_ref=zrecv.at[f, dz],
            send_sem=zsend_sem.at[f, dz], recv_sem=zrecv_sem.at[f, dz],
            device_id=partner, device_id_type=pl.DeviceIdType.MESH,
        )

    def gather(f):
        for dz in range(1, nz):
            z_arrival(f, dz).wait_recv()
        summed = zsend[f, z].astype(jnp.float32)
        for dz in range(1, nz):
            summed = summed + zrecv[f, dz].astype(jnp.float32)
        csum[f] = summed.astype(jnp.bfloat16)

    def head():
        for turn in range(2):
            for dz in range(1, nz):
                h_copy(turn, dz).wait_recv()
            summed = part[(y + 1 - turn) % 2, :, 0, z].astype(jnp.float32)
            for dz in range(1, nz):
                summed = summed + hrecv[turn, dz].astype(jnp.float32)
            hsum[turn] = summed.astype(jnp.bfloat16)
            for k in ((0, 1), (2,))[turn]:
                l_copy(k).start()

    def finish():
        for k in range(3):
            l_copy(k).wait_recv()
        for owner, block, k in ((core, hsum.at[1, core], 0), (1 - core, hlast.at[2], 1)):
            csum[0, owner] = (
                block[...].astype(jnp.float32) + hlast[k].astype(jnp.float32)
            ).astype(jnp.bfloat16)

    def absorb(f):
        source = lax.broadcasted_iota(jnp.int32, (half, lanes), 0)
        outer = (low & (source < WM)) | (~low & (source >= half - WM))
        for owner in range(n_freq):
            block = csum[f, owner]
            index = owner * nf + f
            xr = block[0].astype(jnp.float32)
            xi = block[1].astype(jnp.float32)
            d0 = dat[pl.ds(pl.multiple_of(index * half, half), half), :]
            d1 = dat[pl.ds(pl.multiple_of((NF + index) * half, half), half), :]
            sums = (xr * xr + xi * xi, xr * d0 + xi * d1, xi * d0 - xr * d1)
            for k in range(3):
                every[pl.ds(k * NF + index, 1), :] = jnp.sum(sums[k], 0, keepdims=True)
                edge[pl.ds(k * NF + index, 1), :] = jnp.sum(
                    jnp.where(outer, sums[k], 0.0), 0, keepdims=True
                )
            xt[pl.ds(index, half, stride=2 * NF), :] = xr
            xt[pl.ds(NF + index, half, stride=2 * NF), :] = xi

    def steady(f, carry):
        spec_copy(f).wait()

        @pl.when((f > 0) & (f + DEPTH - 1 < nf))
        def _():
            spec_copy(f + DEPTH - 1).start()

        products(f)

        @pl.when(f == min(HEAD, nf - 1))
        def _():
            head()

        @pl.when(f > LAG)
        def _():
            forward(f - LAG)

        @pl.when(f > LAG + ZLAG)
        def _():
            gather(f - LAG - ZLAG)

        return carry

    for copy in side_copies:
        copy.start()
    lax.fori_loop(0, nf, steady, 0)

    for copy in side_copies:
        copy.wait()
    table = tables[0 : 2 * NF].astype(jnp.bfloat16)
    basis = tables[2 * NF : 4 * NF, :TAPS]
    lags = tables[2 * NF : 4 * NF, lanes : lanes + TAPS]
    gram = tables[4 * NF : 6 * NF, : 2 * NF]
    sel = tables[6 * NF : 6 * NF + 24].astype(jnp.bfloat16)
    basis_halves, lags_halves, gram_halves = halves(basis), halves(lags), halves(gram)
    table_ref[...] = table

    def project(s, carry):
        traces = jnp.concatenate([rec[s], rec[half + s]], 0)
        dat[pl.ds(s, 2 * NF, stride=half), :] = dot_nt(table, traces)
        return carry

    lax.fori_loop(0, half, project, 0, unroll=4)
    start = start_ref[...]
    u0 = dot_nt(start, basis, EXACT)

    def absorb_step(f, carry):
        absorb(f)
        return carry

    ready = max(nf - LAG - ZLAG, 1)
    lax.fori_loop(1, ready, absorb_step, 0)

    def drain(f, carry):
        @pl.when(f < nf)
        def _():
            forward(f)

        @pl.when(f - ZLAG >= 1)
        def _():
            gather(f - ZLAG)
            absorb(f - ZLAG)

        @pl.when(f == nf)
        def _():
            finish()
            absorb(0)

        return carry

    lax.fori_loop(nf - LAG, nf + ZLAG, drain, 0)

    tall = jnp.concatenate([every[:NF], every[...]], 0)
    stat[0, :, : 4 * NF] = dot_nt(sel[:8], split(tall))
    tall = jnp.concatenate([edge[:NF], edge[...]], 0)
    edges = dot_nt(sel[8:], split(tall))
    stat[1, :, : 4 * NF] = edges[:8]
    stat[2, :, : 4 * NF] = edges[8:]

    place = (me + 2 * n_freq) % total
    p, q = place // columns, place % columns

    def halo_copy(j):
        slot = offsets.index((total - offsets[j]) % total)
        if offsets[j] in (1, total - 1):
            kind = 0
        else:
            kind = 1 + jnp.where((place + offsets[j]) % total // columns > p, 1, 0)
        return pltpu.make_async_remote_copy(
            src_ref=stat.at[kind], dst_ref=nrecv.at[slot],
            send_sem=nsend_sem.at[j], recv_sem=nrecv_sem.at[slot],
            device_id=device((me + offsets[j]) % total),
            device_id_type=pl.DeviceIdType.MESH,
        )

    copies = [halo_copy(j) for j in range(len(offsets))]
    for copy in copies[1:-1] + [copies[0], copies[-1]]:
        copy.start()

    def settle(f, carry):
        for piece in range(2):
            for other in range(n_freq):
                y_copy(f, other, piece).wait_send()
        t_copy(f).wait_send()
        for dz in range(1, nz):
            z_copy(f, dz).wait_send()
        return carry

    lax.fori_loop(1, nf, settle, 0)
    for turn in range(2):
        for dz in range(1, nz):
            h_copy(turn, dz).wait_send()
    for k in range(3):
        l_copy(k).wait_send()
    for copy in copies:
        copy.wait_recv()

    windows = stat[0, 0:2, : 4 * NF]
    for dp, dq in directions:
        slot = offsets.index((dp * columns + dq) % total)
        first = {-1: 2, 0: 0, 1: 4}[dq]
        inside = (p + dp >= 0) & (p + dp < rows) & (q + dq >= 0) & (q + dq < columns)
        windows = windows + jnp.where(
            inside, nrecv[slot, first : first + 2, : 4 * NF], 0.0
        )

    power = windows[:, : 2 * NF]
    cross = windows[:, 2 * NF : 4 * NF]
    weight = power * ((NT / 2) * (2.0 / NF))
    residual = cross - weight * u0
    lag_gram = dot_halves(power, lags_halves)
    once = dot_halves(residual, gram_halves)
    twice = dot_halves(weight * once, gram_halves)
    tap = lax.broadcasted_iota(jnp.int32, lag_gram.shape, 1)
    bound = jnp.sum(jnp.where(tap == 0, lag_gram, 2.0 * jnp.abs(lag_gram)), 1, keepdims=True)
    step = 0.5 / (bound + 1e-06)
    v = step * (3.0 * residual - step * (weight * (3.0 * once - step * twice)))
    filters = start + dot_halves(v, basis_halves)
    filters_ref[...] = filters
    taps = filters.astype(jnp.bfloat16)
    response = dot_nt(basis_halves[0], taps) + dot_nt(basis_halves[1], taps)
    window_of = lax.broadcasted_iota(jnp.int32, (NF, lanes), 1) % tr < WC
    hc = jnp.where(window_of, response[:NF, 0:1], response[:NF, 1:2])
    hs = jnp.where(window_of, response[NF:, 0:1], response[NF:, 1:2])

    for s in range(half):
        xr = xt[2 * NF * s : 2 * NF * s + NF]
        xi = xt[2 * NF * s + NF : 2 * NF * (s + 1)]
        shaped = jnp.concatenate([xr * hc + xi * hs, xi * hc - xr * hs], 0)
        shaped_ref[s] = shaped.astype(jnp.bfloat16)

    for copy in copies:
        copy.wait_send()


def subtract(
    shaped_ref, filters_ref, rec, table_ref, primaries_hbm, filters_hbm,
    outv, out_sem, filters_sem,
):
    half, tr = shaped_ref.shape[0], rec.shape[1]
    group = half // out_sem.shape[0]
    filters_copy = pltpu.make_async_copy(filters_ref, filters_hbm, filters_sem)
    filters_copy.start()
    copies = []
    for s in range(half):
        predicted = lax.dot_general(
            shaped_ref[s], table_ref[...], (((0,), (0,)), ((), ())),
            preferred_element_type=jnp.float32,
        )
        outv[s] = (rec[s].astype(jnp.float32) - predicted[:tr]).astype(jnp.bfloat16)
        outv[half + s] = (
            rec[half + s].astype(jnp.float32) - predicted[tr:]
        ).astype(jnp.bfloat16)
        if s % group == group - 1:
            for h in range(2):
                span = pl.ds(h * half + s - group + 1, group)
                copy = pltpu.make_async_copy(
                    outv.at[span], primaries_hbm.at[span], out_sem.at[s // group, h]
                )
                copy.start()
                copies.append(copy)
    for copy in copies + [filters_copy]:
        copy.wait()


def body(mesh_shape, spectra, recorded, initial_filters):
    n_refl, n_freq = mesh_shape["refl"], mesh_shape["freq"]
    nf, receivers, points = spectra.shape[1:]
    ts, tr, samples = recorded.shape[2:]
    sources = ts * (n_refl // 4)
    nz = n_refl // 2
    half, lanes = ts // 2, 2 * tr
    total, columns = n_refl * n_freq, 4 * n_freq
    n_halo = len(
        {(dp * columns + dq) % total for dp in (-1, 0, 1) for dq in (-1, 0, 1)} - {0}
    )
    basis, gram, lags = filter_tables()
    vmem = pl.BlockSpec(memory_space=pltpu.VMEM)
    hbm = pl.BlockSpec(memory_space=pltpu.HBM)
    tables = np.zeros((6 * NF + 24, max(samples, 2 * lanes)), np.float32)
    tables[: 2 * NF, :samples] = time_rows().astype(ml_dtypes.bfloat16).astype(np.float32)
    tables[2 * NF : 4 * NF, :TAPS] = basis
    tables[2 * NF : 4 * NF, lanes : lanes + TAPS] = lags
    tables[4 * NF : 6 * NF, : 2 * NF] = gram
    tables[6 * NF :] = lane_selection(tr)
    bf16, f32 = jnp.bfloat16, jnp.float32
    staged = pl.pallas_call(
        functools.partial(kernel, n_refl, n_freq, sources),
        out_shape=(
            jax.ShapeDtypeStruct((half, 2 * NF, lanes), bf16),
            jax.ShapeDtypeStruct((2, TAPS), f32),
            jax.ShapeDtypeStruct((ts, tr, samples), bf16),
            jax.ShapeDtypeStruct((2 * NF, samples), bf16),
        ),
        in_specs=[hbm] * 4,
        out_specs=(vmem,) * 4,
        scratch_shapes=[
            pltpu.VMEM((2, TAPS), f32),
            pltpu.VMEM(tables.shape, f32),
            pltpu.VMEM((nf, 2, receivers, points), bf16),
            pltpu.VMEM((2, n_freq, nf, nz, 2, half, lanes), bf16),
            pltpu.VMEM((n_freq, nf, nz, 2, half, lanes), bf16),
            pltpu.VMEM((nf, nz, 2, half, lanes), bf16),
            pltpu.VMEM((nf, nz, n_freq, 2, half, lanes), bf16),
            pltpu.VMEM((nf, nz, n_freq, 2, half, lanes), bf16),
            pltpu.VMEM((2, nz, n_freq, 2, half, lanes), bf16),
            pltpu.VMEM((2, n_freq, 2, half, lanes), bf16),
            pltpu.VMEM((3, 2, half, lanes), bf16),
            pltpu.VMEM((nf, n_freq, 2, half, lanes), bf16),
            pltpu.VMEM((2 * NF * half, lanes), f32),
            pltpu.VMEM((half * 2 * NF, lanes), f32),
            pltpu.VMEM((3 * NF, lanes), f32),
            pltpu.VMEM((3 * NF, lanes), f32),
            pltpu.VMEM((3, 8, lanes), f32),
            pltpu.VMEM((n_halo, 8, lanes), f32),
            pltpu.SemaphoreType.DMA((nf,)),
            pltpu.SemaphoreType.DMA,
            pltpu.SemaphoreType.DMA,
            pltpu.SemaphoreType.DMA,
            pltpu.SemaphoreType.DMA((nf, 2, n_freq)),
            pltpu.SemaphoreType.DMA((nf, 2, n_freq)),
            pltpu.SemaphoreType.DMA((nf, nz)),
            pltpu.SemaphoreType.DMA((nf, nz)),
            pltpu.SemaphoreType.DMA((nf,)),
            pltpu.SemaphoreType.DMA((nf,)),
            pltpu.SemaphoreType.DMA((2, nz)),
            pltpu.SemaphoreType.DMA((2, nz)),
            pltpu.SemaphoreType.DMA((3,)),
            pltpu.SemaphoreType.DMA((3,)),
            pltpu.SemaphoreType.DMA((n_halo,)),
            pltpu.SemaphoreType.DMA((n_halo,)),
        ],
        compiler_params=pltpu.CompilerParams(
            collective_id=0, has_side_effects=True, vmem_limit_bytes=40 * 1024 * 1024
        ),
    )(
        *[
            pltpu.with_memory_space_constraint(x, pltpu.HBM)
            for x in (
                spectra,
                recorded.reshape(ts, tr, samples),
                initial_filters.reshape(2, TAPS),
                jnp.asarray(tables),
            )
        ]
    )
    primaries, filters = pl.pallas_call(
        subtract,
        out_shape=(
            jax.ShapeDtypeStruct((ts, tr, samples), bf16),
            jax.ShapeDtypeStruct((2, TAPS), f32),
        ),
        in_specs=[vmem] * 4,
        out_specs=(hbm, hbm),
        scratch_shapes=[
            pltpu.VMEM((ts, tr, samples), bf16),
            pltpu.SemaphoreType.DMA((4, 2)),
            pltpu.SemaphoreType.DMA,
        ],
        compiler_params=pltpu.CompilerParams(vmem_limit_bytes=40 * 1024 * 1024),
    )(*staged)
    return (
        primaries.reshape(recorded.shape),
        filters.reshape(initial_filters.shape),
    )


def solution(mesh):
    placed = (
        P(None, "freq", "groups", "refl"),
        P("refl", "freq", "groups", None, None),
        P("refl", "freq", "groups", None, None),
    )
    return jax.shard_map(
        functools.partial(body, dict(mesh.shape)),
        mesh=mesh,
        in_specs=placed,
        out_specs=(
            P("refl", "freq", "groups", None, None),
            P("refl", "freq", "groups", None, None),
        ),
        check_vma=False,
    )
```

```python
import functools
import math

import jax
import jax.numpy as jnp
import ml_dtypes
import numpy as np
from jax import lax
from jax.experimental import pallas as pl
from jax.experimental.pallas import tpu as pltpu
from jax.sharding import PartitionSpec as P

NF = 16
K0 = 48
NT = 256
XR = 8192
WC = 32
WM = 4
TAPS = 33
HALF = (TAPS - 1) // 2
LAG = 2
ZLAG = 3
DEPTH = 4
HEAD = 7
EXACT = lax.Precision.HIGHEST


def angles_of(steps):
    bins = K0 + np.arange(NF)
    return 2.0 * math.pi / NT * ((bins[:, None] * steps[None, :]) % NT)


def time_rows():
    angles = angles_of(np.arange(NT))
    weight = math.sqrt(2.0 / NF)
    return np.concatenate([weight * np.cos(angles), -weight * np.sin(angles)], 0)


def filter_tables():
    tap_angles = angles_of(np.arange(TAPS) - HALF)
    basis = np.concatenate([np.cos(tap_angles), np.sin(tap_angles)], 0)
    lags = np.cos(angles_of(np.arange(TAPS))) * (NT / 2) * (2.0 / NF)
    lags = np.concatenate([lags, np.zeros_like(lags)], 0)
    return basis, basis @ basis.T, lags


def lane_selection(tr):
    lane = np.arange(2 * tr)
    receiver = lane % tr
    rows = np.zeros((3, 8, 2 * tr), np.float32)
    for kind, within in enumerate((lane >= 0, lane < tr, lane >= tr)):
        rows[kind, 0] = within & (receiver < WC + WM)
        rows[kind, 1] = within & (receiver >= tr - WC - WM)
        rows[kind, 2] = within & (receiver >= tr - WM)
        rows[kind, 5] = within & (receiver < WM)
    rows = rows.reshape(24, 2 * tr)
    return np.concatenate([rows, rows], 1)


def dot_nt(a, b, precision=None):
    return lax.dot_general(
        a, b, (((1,), (1,)), ((), ())), precision=precision,
        preferred_element_type=jnp.float32,
    )


def dot_nn(a, b, precision=None):
    return lax.dot_general(
        a, b, (((1,), (0,)), ((), ())), precision=precision,
        preferred_element_type=jnp.float32,
    )


def split(x):
    high = x.astype(jnp.bfloat16)
    low = (x - high.astype(jnp.float32)).astype(jnp.bfloat16)
    return jnp.concatenate([high, low], 1)


def halves(x):
    high = x.astype(jnp.bfloat16)
    return high, (x - high.astype(jnp.float32)).astype(jnp.bfloat16)


def dot_halves(x, table):
    high, low = halves(x)
    return dot_nn(high, table[0]) + (dot_nn(low, table[0]) + dot_nn(high, table[1]))


def kernel(
    n_refl, n_freq, sources,
    spectra_hbm, recorded_hbm, start_hbm, tables_hbm,
    shaped_ref, filters_ref, rec, table_ref,
    start_ref, tables, spec, part, yrecv, trecv, zsend, zrecv, hrecv, hsum, hlast, csum, dat, xt, every, edge,
    stat, nrecv,
    spec_sem, rec_sem, start_sem, tables_sem, ysend_sem, yrecv_sem, zsend_sem, zrecv_sem,
    tsend_sem, trecv_sem, hsend_sem, hrecv_sem,
    lsend_sem, lrecv_sem, nsend_sem, nrecv_sem,
):
    nf = spec.shape[0]
    ts, tr = rec.shape[0], rec.shape[1]
    half = ts // 2
    lanes = 2 * tr
    nz = n_refl // 2
    total = n_refl * n_freq
    columns = 4 * n_freq
    rows = total // columns
    amplitude = 1.0 / math.sqrt(2.0 * XR)
    refl = lax.axis_index("refl")
    core = lax.axis_index("freq")
    me = refl * n_freq + core
    z = refl // 2
    y = refl % 2
    partner = {"refl": z * 2 + (1 - y), "freq": core}
    twin = {"refl": refl, "freq": 1 - core}

    def device(linear):
        return {"refl": linear // n_freq, "freq": linear % n_freq}

    def spec_copy(f):
        return pltpu.make_async_copy(spectra_hbm.at[:, f], spec.at[f], spec_sem.at[f])

    side_copies = [
        pltpu.make_async_copy(recorded_hbm, rec, rec_sem),
        pltpu.make_async_copy(tables_hbm, tables, tables_sem),
        pltpu.make_async_copy(start_hbm, start_ref, start_sem),
    ]

    for f in range(DEPTH):
        spec_copy(f).start()

    barrier = pltpu.get_barrier_semaphore()

    directions = [(dp, dq) for dp in (-1, 0, 1) for dq in (-1, 0, 1) if dp or dq]
    offsets = sorted({(dp * columns + dq) % total for dp, dq in directions} - {0})
    met = [partner, twin, {"refl": z * 2 + (1 - y), "freq": 1 - core}]
    met += [{"refl": (z + dz) % nz * 2 + y, "freq": core} for dz in range(1, nz)]
    met += [device((me + offset) % total) for offset in offsets]
    for peer in met:
        pl.semaphore_signal(
            barrier, inc=1, device_id=peer, device_id_type=pl.DeviceIdType.MESH
        )

    lane = lax.broadcasted_iota(jnp.int32, (half, lanes), 1)
    low = lane < tr

    def y_copy(f, other, turn):
        to = (core + other) % 2
        span = pl.ds(turn * (nz // 2), nz // 2)
        return pltpu.make_async_remote_copy(
            src_ref=part.at[1 - y, to, f, span], dst_ref=yrecv.at[core, f, span],
            send_sem=ysend_sem.at[f, turn, other], recv_sem=yrecv_sem.at[f, turn, core],
            device_id={"refl": z * 2 + (1 - y), "freq": to},
            device_id_type=pl.DeviceIdType.MESH,
        )

    def y_arrival(f, sender, turn):
        span = pl.ds(turn * (nz // 2), nz // 2)
        return pltpu.make_async_remote_copy(
            src_ref=part.at[1 - y, core, f, span], dst_ref=yrecv.at[sender, f, span],
            send_sem=ysend_sem.at[f, turn, 0], recv_sem=yrecv_sem.at[f, turn, sender],
            device_id=partner, device_id_type=pl.DeviceIdType.MESH,
        )

    def t_copy(f):
        return pltpu.make_async_remote_copy(
            src_ref=part.at[y, 1 - core, f], dst_ref=trecv.at[f],
            send_sem=tsend_sem.at[f], recv_sem=trecv_sem.at[f],
            device_id=twin, device_id_type=pl.DeviceIdType.MESH,
        )

    def z_copy(f, dz):
        to_z = (z + dz) % nz
        return pltpu.make_async_remote_copy(
            src_ref=zsend.at[f, to_z], dst_ref=zrecv.at[f, dz],
            send_sem=zsend_sem.at[f, dz], recv_sem=zrecv_sem.at[f, dz],
            device_id={"refl": to_z * 2 + y, "freq": core},
            device_id_type=pl.DeviceIdType.MESH,
        )

    def h_copy(turn, dz):
        to_z = (z + dz) % nz
        parity = (y + 1 - turn) % 2
        return pltpu.make_async_remote_copy(
            src_ref=part.at[parity, :, 0, to_z], dst_ref=hrecv.at[turn, dz],
            send_sem=hsend_sem.at[turn, dz], recv_sem=hrecv_sem.at[turn, dz],
            device_id={"refl": to_z * 2 + y, "freq": core},
            device_id_type=pl.DeviceIdType.MESH,
        )

    def l_copy(k):
        to = core if k == 0 else 1 - core
        return pltpu.make_async_remote_copy(
            src_ref=hsum.at[k // 2, to], dst_ref=hlast.at[k],
            send_sem=lsend_sem.at[k], recv_sem=lrecv_sem.at[k],
            device_id=(partner, met[2], twin)[k], device_id_type=pl.DeviceIdType.MESH,
        )

    def products(f):
        real = spec[f, 0, :sources] * jnp.bfloat16(amplitude)
        imag = spec[f, 1, :sources] * jnp.bfloat16(amplitude)
        by_real = jnp.concatenate([real, imag], 0)
        by_imag = jnp.concatenate([-imag, real], 0)
        def one(turn, carry):
            parity = (1 - y) * (1 - turn) + y * turn
            spans = [
                pl.ds(pl.multiple_of((parity + 2 * g) * lanes, lanes), lanes)
                for g in range(2)
            ]
            terms = dot_nt(
                jnp.concatenate([by_real, by_imag], 1),
                jnp.concatenate(
                    [jnp.concatenate([spec[f, c, span] for c in range(2)], 1) for span in spans], 0
                ),
            )
            for g in range(2):
                for p in range(n_refl // 4):
                    to_z = (4 * p + 2 * g - 2) % n_refl // 2
                    for c in range(2):
                        row = c * sources + p * ts
                        a = terms[row : row + half, g * lanes : (g + 1) * lanes]
                        b = terms[row + half : row + ts, g * lanes : (g + 1) * lanes]
                        turned = pltpu.roll(jnp.where(low, b, a), tr, 1)
                        part[parity, 0, f, to_z, c] = jnp.where(low, a, turned).astype(
                            jnp.bfloat16
                        )
                        part[parity, 1, f, to_z, c] = jnp.where(low, turned, b).astype(
                            jnp.bfloat16
                        )
            @pl.when((turn == 0) & (f == 0))
            def _():
                pl.semaphore_wait(barrier, len(met))

            @pl.when(f == 0)
            def _():
                for dz in range(1, nz):
                    h_copy(turn, dz).start()

            @pl.when((turn == 0) & (f > 0))
            def _():
                for piece in range(2):
                    for other in range(n_freq):
                        y_copy(f, other, piece).start()

            @pl.when((turn == 1) & (f > 0))
            def _():
                t_copy(f).start()

            return carry

        lax.fori_loop(0, 2, one, 0)

    def forward(f):
        t_copy(f).wait_recv()
        for piece in range(2):
            for sender in range(n_freq):
                y_arrival(f, sender, piece).wait_recv()
            span = slice(piece * (nz // 2), (piece + 1) * (nz // 2))
            for owner, block in ((core, part.at[y, core, f]), (1 - core, trecv.at[f])):
                zsend[f, span, owner] = (
                    block[span].astype(jnp.float32) + yrecv[owner, f, span].astype(jnp.float32)
                ).astype(jnp.bfloat16)
            for n in range(nz // 2):
                to_z = piece * (nz // 2) + (n if piece == 0 else nz // 2 - 1 - n)
                @pl.when(z != to_z)
                def _():
                    z_copy(f, (to_z - z + nz) % nz).start()

    def z_arrival(f, dz):
        return pltpu.make_async_remote_copy(
            src_ref=zsend.at[f, z], dst_ref=zrecv.at[f, dz],
            send_sem=zsend_sem.at[f, dz], recv_sem=zrecv_sem.at[f, dz],
            device_id=partner, device_id_type=pl.DeviceIdType.MESH,
        )

    def gather(f):
        for dz in range(1, nz):
            z_arrival(f, dz).wait_recv()
        summed = zsend[f, z].astype(jnp.float32)
        for dz in range(1, nz):
            summed = summed + zrecv[f, dz].astype(jnp.float32)
        csum[f] = summed.astype(jnp.bfloat16)

    def head():
        for turn in range(2):
            for dz in range(1, nz):
                h_copy(turn, dz).wait_recv()
            summed = part[(y + 1 - turn) % 2, :, 0, z].astype(jnp.float32)
            for dz in range(1, nz):
                summed = summed + hrecv[turn, dz].astype(jnp.float32)
            hsum[turn] = summed.astype(jnp.bfloat16)
            for k in ((0, 1), (2,))[turn]:
                l_copy(k).start()

    def finish():
        for k in range(3):
            l_copy(k).wait_recv()
        for owner, block, k in ((core, hsum.at[1, core], 0), (1 - core, hlast.at[2], 1)):
            csum[0, owner] = (
                block[...].astype(jnp.float32) + hlast[k].astype(jnp.float32)
            ).astype(jnp.bfloat16)

    def absorb(f):
        source = lax.broadcasted_iota(jnp.int32, (half, lanes), 0)
        outer = (low & (source < WM)) | (~low & (source >= half - WM))
        for owner in range(n_freq):
            block = csum[f, owner]
            index = owner * nf + f
            xr = block[0].astype(jnp.float32)
            xi = block[1].astype(jnp.float32)
            d0 = dat[pl.ds(pl.multiple_of(index * half, half), half), :]
            d1 = dat[pl.ds(pl.multiple_of((NF + index) * half, half), half), :]
            sums = (xr * xr + xi * xi, xr * d0 + xi * d1, xi * d0 - xr * d1)
            for k in range(3):
                every[pl.ds(k * NF + index, 1), :] = jnp.sum(sums[k], 0, keepdims=True)
                edge[pl.ds(k * NF + index, 1), :] = jnp.sum(
                    jnp.where(outer, sums[k], 0.0), 0, keepdims=True
                )
            xt[pl.ds(index, half, stride=2 * NF), :] = xr
            xt[pl.ds(NF + index, half, stride=2 * NF), :] = xi

    def steady(f, carry):
        spec_copy(f).wait()

        @pl.when((f > 0) & (f + DEPTH - 1 < nf))
        def _():
            spec_copy(f + DEPTH - 1).start()

        products(f)

        @pl.when(f == min(HEAD, nf - 1))
        def _():
            head()

        @pl.when(f > LAG)
        def _():
            forward(f - LAG)

        @pl.when(f > LAG + ZLAG)
        def _():
            gather(f - LAG - ZLAG)

        return carry

    for copy in side_copies:
        copy.start()
    lax.fori_loop(0, nf, steady, 0)

    forward(nf - LAG)
    for copy in side_copies:
        copy.wait()
    table = tables[0 : 2 * NF].astype(jnp.bfloat16)
    basis = tables[2 * NF : 4 * NF, :TAPS]
    lags = tables[2 * NF : 4 * NF, lanes : lanes + TAPS]
    gram = tables[4 * NF : 6 * NF, : 2 * NF]
    sel = tables[6 * NF : 6 * NF + 24].astype(jnp.bfloat16)
    basis_halves, lags_halves, gram_halves = halves(basis), halves(lags), halves(gram)
    table_ref[...] = table

    def project(s, carry):
        traces = jnp.concatenate([rec[s], rec[half + s]], 0)
        dat[pl.ds(s, 2 * NF, stride=half), :] = dot_nt(table, traces)
        return carry

    lax.fori_loop(0, half, project, 0, unroll=4)
    start = start_ref[...]
    u0 = dot_nt(start, basis, EXACT)

    def absorb_step(f, carry):
        absorb(f)
        return carry

    ready = max(nf - LAG - ZLAG, 1)
    lax.fori_loop(1, ready, absorb_step, 0)

    def drain(f, carry):
        @pl.when((f > nf - LAG) & (f < nf))
        def _():
            forward(f)

        @pl.when(f - ZLAG >= 1)
        def _():
            gather(f - ZLAG)
            absorb(f - ZLAG)

        @pl.when(f == nf)
        def _():
            finish()
            absorb(0)

        return carry

    lax.fori_loop(nf - LAG, nf + ZLAG, drain, 0)

    tall = jnp.concatenate([every[:NF], every[...]], 0)
    stat[0, :, : 4 * NF] = dot_nt(sel[:8], split(tall))
    tall = jnp.concatenate([edge[:NF], edge[...]], 0)
    edges = dot_nt(sel[8:], split(tall))
    stat[1, :, : 4 * NF] = edges[:8]
    stat[2, :, : 4 * NF] = edges[8:]

    place = (me + 2 * n_freq) % total
    p, q = place // columns, place % columns

    def halo_copy(j):
        slot = offsets.index((total - offsets[j]) % total)
        if offsets[j] in (1, total - 1):
            kind = 0
        else:
            kind = 1 + jnp.where((place + offsets[j]) % total // columns > p, 1, 0)
        return pltpu.make_async_remote_copy(
            src_ref=stat.at[kind], dst_ref=nrecv.at[slot],
            send_sem=nsend_sem.at[j], recv_sem=nrecv_sem.at[slot],
            device_id=device((me + offsets[j]) % total),
            device_id_type=pl.DeviceIdType.MESH,
        )

    copies = [halo_copy(j) for j in range(len(offsets))]
    for copy in copies[1:-1] + [copies[0], copies[-1]]:
        copy.start()

    def settle(f, carry):
        for piece in range(2):
            for other in range(n_freq):
                y_copy(f, other, piece).wait_send()
        t_copy(f).wait_send()
        for dz in range(1, nz):
            z_copy(f, dz).wait_send()
        return carry

    lax.fori_loop(1, nf, settle, 0)
    for turn in range(2):
        for dz in range(1, nz):
            h_copy(turn, dz).wait_send()
    for k in range(3):
        l_copy(k).wait_send()
    for copy in copies:
        copy.wait_recv()

    windows = stat[0, 0:2, : 4 * NF]
    for dp, dq in directions:
        slot = offsets.index((dp * columns + dq) % total)
        first = {-1: 2, 0: 0, 1: 4}[dq]
        inside = (p + dp >= 0) & (p + dp < rows) & (q + dq >= 0) & (q + dq < columns)
        windows = windows + jnp.where(
            inside, nrecv[slot, first : first + 2, : 4 * NF], 0.0
        )

    power = windows[:, : 2 * NF]
    cross = windows[:, 2 * NF : 4 * NF]
    weight = power * ((NT / 2) * (2.0 / NF))
    residual = cross - weight * u0
    lag_gram = dot_halves(power, lags_halves)
    once = dot_halves(residual, gram_halves)
    twice = dot_halves(weight * once, gram_halves)
    tap = lax.broadcasted_iota(jnp.int32, lag_gram.shape, 1)
    bound = jnp.sum(jnp.where(tap == 0, lag_gram, 2.0 * jnp.abs(lag_gram)), 1, keepdims=True)
    step = 0.5 / (bound + 1e-06)
    v = step * (3.0 * residual - step * (weight * (3.0 * once - step * twice)))
    filters = start + dot_halves(v, basis_halves)
    filters_ref[...] = filters
    taps = filters.astype(jnp.bfloat16)
    response = dot_nt(basis_halves[0], taps) + dot_nt(basis_halves[1], taps)
    window_of = lax.broadcasted_iota(jnp.int32, (NF, lanes), 1) % tr < WC
    hc = jnp.where(window_of, response[:NF, 0:1], response[:NF, 1:2])
    hs = jnp.where(window_of, response[NF:, 0:1], response[NF:, 1:2])

    for s in range(half):
        xr = xt[2 * NF * s : 2 * NF * s + NF]
        xi = xt[2 * NF * s + NF : 2 * NF * (s + 1)]
        shaped = jnp.concatenate([xr * hc + xi * hs, xi * hc - xr * hs], 0)
        shaped_ref[s] = shaped.astype(jnp.bfloat16)

    for copy in copies:
        copy.wait_send()


def subtract(
    shaped_ref, filters_ref, rec, table_ref, primaries_hbm, filters_hbm,
    outv, out_sem, filters_sem,
):
    half, tr = shaped_ref.shape[0], rec.shape[1]
    group = half // out_sem.shape[0]
    filters_copy = pltpu.make_async_copy(filters_ref, filters_hbm, filters_sem)
    filters_copy.start()
    copies = []
    for s in range(half):
        predicted = lax.dot_general(
            shaped_ref[s], table_ref[...], (((0,), (0,)), ((), ())),
            preferred_element_type=jnp.float32,
        )
        outv[s] = (rec[s].astype(jnp.float32) - predicted[:tr]).astype(jnp.bfloat16)
        outv[half + s] = (
            rec[half + s].astype(jnp.float32) - predicted[tr:]
        ).astype(jnp.bfloat16)
        if s % group == group - 1:
            for h in range(2):
                span = pl.ds(h * half + s - group + 1, group)
                copy = pltpu.make_async_copy(
                    outv.at[span], primaries_hbm.at[span], out_sem.at[s // group, h]
                )
                copy.start()
                copies.append(copy)
    for copy in copies + [filters_copy]:
        copy.wait()


def body(mesh_shape, spectra, recorded, initial_filters):
    n_refl, n_freq = mesh_shape["refl"], mesh_shape["freq"]
    nf, receivers, points = spectra.shape[1:]
    ts, tr, samples = recorded.shape[2:]
    sources = ts * (n_refl // 4)
    nz = n_refl // 2
    half, lanes = ts // 2, 2 * tr
    total, columns = n_refl * n_freq, 4 * n_freq
    n_halo = len(
        {(dp * columns + dq) % total for dp in (-1, 0, 1) for dq in (-1, 0, 1)} - {0}
    )
    basis, gram, lags = filter_tables()
    vmem = pl.BlockSpec(memory_space=pltpu.VMEM)
    hbm = pl.BlockSpec(memory_space=pltpu.HBM)
    tables = np.zeros((6 * NF + 24, max(samples, 2 * lanes)), np.float32)
    tables[: 2 * NF, :samples] = time_rows().astype(ml_dtypes.bfloat16).astype(np.float32)
    tables[2 * NF : 4 * NF, :TAPS] = basis
    tables[2 * NF : 4 * NF, lanes : lanes + TAPS] = lags
    tables[4 * NF : 6 * NF, : 2 * NF] = gram
    tables[6 * NF :] = lane_selection(tr)
    bf16, f32 = jnp.bfloat16, jnp.float32
    staged = pl.pallas_call(
        functools.partial(kernel, n_refl, n_freq, sources),
        out_shape=(
            jax.ShapeDtypeStruct((half, 2 * NF, lanes), bf16),
            jax.ShapeDtypeStruct((2, TAPS), f32),
            jax.ShapeDtypeStruct((ts, tr, samples), bf16),
            jax.ShapeDtypeStruct((2 * NF, samples), bf16),
        ),
        in_specs=[hbm] * 4,
        out_specs=(vmem,) * 4,
        scratch_shapes=[
            pltpu.VMEM((2, TAPS), f32),
            pltpu.VMEM(tables.shape, f32),
            pltpu.VMEM((nf, 2, receivers, points), bf16),
            pltpu.VMEM((2, n_freq, nf, nz, 2, half, lanes), bf16),
            pltpu.VMEM((n_freq, nf, nz, 2, half, lanes), bf16),
            pltpu.VMEM((nf, nz, 2, half, lanes), bf16),
            pltpu.VMEM((nf, nz, n_freq, 2, half, lanes), bf16),
            pltpu.VMEM((nf, nz, n_freq, 2, half, lanes), bf16),
            pltpu.VMEM((2, nz, n_freq, 2, half, lanes), bf16),
            pltpu.VMEM((2, n_freq, 2, half, lanes), bf16),
            pltpu.VMEM((3, 2, half, lanes), bf16),
            pltpu.VMEM((nf, n_freq, 2, half, lanes), bf16),
            pltpu.VMEM((2 * NF * half, lanes), f32),
            pltpu.VMEM((half * 2 * NF, lanes), f32),
            pltpu.VMEM((3 * NF, lanes), f32),
            pltpu.VMEM((3 * NF, lanes), f32),
            pltpu.VMEM((3, 8, lanes), f32),
            pltpu.VMEM((n_halo, 8, lanes), f32),
            pltpu.SemaphoreType.DMA((nf,)),
            pltpu.SemaphoreType.DMA,
            pltpu.SemaphoreType.DMA,
            pltpu.SemaphoreType.DMA,
            pltpu.SemaphoreType.DMA((nf, 2, n_freq)),
            pltpu.SemaphoreType.DMA((nf, 2, n_freq)),
            pltpu.SemaphoreType.DMA((nf, nz)),
            pltpu.SemaphoreType.DMA((nf, nz)),
            pltpu.SemaphoreType.DMA((nf,)),
            pltpu.SemaphoreType.DMA((nf,)),
            pltpu.SemaphoreType.DMA((2, nz)),
            pltpu.SemaphoreType.DMA((2, nz)),
            pltpu.SemaphoreType.DMA((3,)),
            pltpu.SemaphoreType.DMA((3,)),
            pltpu.SemaphoreType.DMA((n_halo,)),
            pltpu.SemaphoreType.DMA((n_halo,)),
        ],
        compiler_params=pltpu.CompilerParams(
            collective_id=0, has_side_effects=True, vmem_limit_bytes=40 * 1024 * 1024
        ),
    )(
        *[
            pltpu.with_memory_space_constraint(x, pltpu.HBM)
            for x in (
                spectra,
                recorded.reshape(ts, tr, samples),
                initial_filters.reshape(2, TAPS),
                jnp.asarray(tables),
            )
        ]
    )
    primaries, filters = pl.pallas_call(
        subtract,
        out_shape=(
            jax.ShapeDtypeStruct((ts, tr, samples), bf16),
            jax.ShapeDtypeStruct((2, TAPS), f32),
        ),
        in_specs=[vmem] * 4,
        out_specs=(hbm, hbm),
        scratch_shapes=[
            pltpu.VMEM((ts, tr, samples), bf16),
            pltpu.SemaphoreType.DMA((4, 2)),
            pltpu.SemaphoreType.DMA,
        ],
        compiler_params=pltpu.CompilerParams(vmem_limit_bytes=40 * 1024 * 1024),
    )(*staged)
    return (
        primaries.reshape(recorded.shape),
        filters.reshape(initial_filters.shape),
    )


def solution(mesh):
    placed = (
        P(None, "freq", "groups", "refl"),
        P("refl", "freq", "groups", None, None),
        P("refl", "freq", "groups", None, None),
    )
    return jax.shard_map(
        functools.partial(body, dict(mesh.shape)),
        mesh=mesh,
        in_specs=placed,
        out_specs=(
            P("refl", "freq", "groups", None, None),
            P("refl", "freq", "groups", None, None),
        ),
        check_vma=False,
    )
```

```python
import functools
import math

import jax
import jax.numpy as jnp
import ml_dtypes
import numpy as np
from jax import lax
from jax.experimental import pallas as pl
from jax.experimental.pallas import tpu as pltpu
from jax.sharding import PartitionSpec as P

NF = 16
K0 = 48
NT = 256
XR = 8192
WC = 32
WM = 4
TAPS = 33
HALF = (TAPS - 1) // 2
LAG = 2
ZLAG = 3
DEPTH = 3
HEAD = 7
EXACT = lax.Precision.HIGHEST


def angles_of(steps):
    bins = K0 + np.arange(NF)
    return 2.0 * math.pi / NT * ((bins[:, None] * steps[None, :]) % NT)


def time_rows():
    angles = angles_of(np.arange(NT))
    weight = math.sqrt(2.0 / NF)
    return np.concatenate([weight * np.cos(angles), -weight * np.sin(angles)], 0)


def filter_tables():
    tap_angles = angles_of(np.arange(TAPS) - HALF)
    basis = np.concatenate([np.cos(tap_angles), np.sin(tap_angles)], 0)
    lags = np.cos(angles_of(np.arange(TAPS))) * (NT / 2) * (2.0 / NF)
    lags = np.concatenate([lags, np.zeros_like(lags)], 0)
    return basis, basis @ basis.T, lags


def lane_selection(tr):
    lane = np.arange(2 * tr)
    receiver = lane % tr
    rows = np.zeros((3, 8, 2 * tr), np.float32)
    for kind, within in enumerate((lane >= 0, lane < tr, lane >= tr)):
        rows[kind, 0] = within & (receiver < WC + WM)
        rows[kind, 1] = within & (receiver >= tr - WC - WM)
        rows[kind, 2] = within & (receiver >= tr - WM)
        rows[kind, 5] = within & (receiver < WM)
    rows = rows.reshape(24, 2 * tr)
    return np.concatenate([rows, rows], 1)


def dot_nt(a, b, precision=None):
    return lax.dot_general(
        a, b, (((1,), (1,)), ((), ())), precision=precision,
        preferred_element_type=jnp.float32,
    )


def dot_nn(a, b, precision=None):
    return lax.dot_general(
        a, b, (((1,), (0,)), ((), ())), precision=precision,
        preferred_element_type=jnp.float32,
    )


def split(x):
    high = x.astype(jnp.bfloat16)
    low = (x - high.astype(jnp.float32)).astype(jnp.bfloat16)
    return jnp.concatenate([high, low], 1)


def halves(x):
    high = x.astype(jnp.bfloat16)
    return high, (x - high.astype(jnp.float32)).astype(jnp.bfloat16)


def dot_halves(x, table):
    high, low = halves(x)
    return dot_nn(high, table[0]) + (dot_nn(low, table[0]) + dot_nn(high, table[1]))


def kernel(
    n_refl, n_freq, sources,
    spectra_hbm, recorded_hbm, start_hbm, tables_hbm,
    shaped_ref, filters_ref, rec, table_ref,
    start_ref, tables, spec, part, yrecv, trecv, zsend, zrecv, hrecv, hsum, hlast, csum, dat, xt, every, edge,
    stat, nrecv,
    spec_sem, rec_sem, start_sem, tables_sem, ysend_sem, yrecv_sem, zsend_sem, zrecv_sem,
    tsend_sem, trecv_sem, hsend_sem, hrecv_sem,
    lsend_sem, lrecv_sem, nsend_sem, nrecv_sem,
):
    nf = spec.shape[0]
    ts, tr = rec.shape[0], rec.shape[1]
    half = ts // 2
    lanes = 2 * tr
    nz = n_refl // 2
    total = n_refl * n_freq
    columns = 4 * n_freq
    rows = total // columns
    amplitude = 1.0 / math.sqrt(2.0 * XR)
    refl = lax.axis_index("refl")
    core = lax.axis_index("freq")
    me = refl * n_freq + core
    z = refl // 2
    y = refl % 2
    partner = {"refl": z * 2 + (1 - y), "freq": core}
    twin = {"refl": refl, "freq": 1 - core}

    def device(linear):
        return {"refl": linear // n_freq, "freq": linear % n_freq}

    def spec_copy(f):
        return pltpu.make_async_copy(spectra_hbm.at[:, f], spec.at[f], spec_sem.at[f])

    side_copies = [
        pltpu.make_async_copy(recorded_hbm, rec, rec_sem),
        pltpu.make_async_copy(tables_hbm, tables, tables_sem),
        pltpu.make_async_copy(start_hbm, start_ref, start_sem),
    ]

    for f in range(DEPTH):
        spec_copy(f).start()

    barrier = pltpu.get_barrier_semaphore()

    directions = [(dp, dq) for dp in (-1, 0, 1) for dq in (-1, 0, 1) if dp or dq]
    offsets = sorted({(dp * columns + dq) % total for dp, dq in directions} - {0})
    met = [partner, twin, {"refl": z * 2 + (1 - y), "freq": 1 - core}]
    met += [{"refl": (z + dz) % nz * 2 + y, "freq": core} for dz in range(1, nz)]
    met += [device((me + offset) % total) for offset in offsets]
    for peer in met:
        pl.semaphore_signal(
            barrier, inc=1, device_id=peer, device_id_type=pl.DeviceIdType.MESH
        )

    lane = lax.broadcasted_iota(jnp.int32, (half, lanes), 1)
    low = lane < tr

    def y_copy(f, other, turn):
        to = (core + other) % 2
        span = pl.ds(turn * (nz // 2), nz // 2)
        return pltpu.make_async_remote_copy(
            src_ref=part.at[1 - y, to, f, span], dst_ref=yrecv.at[core, f, span],
            send_sem=ysend_sem.at[f, turn, other], recv_sem=yrecv_sem.at[f, turn, core],
            device_id={"refl": z * 2 + (1 - y), "freq": to},
            device_id_type=pl.DeviceIdType.MESH,
        )

    def y_arrival(f, sender, turn):
        span = pl.ds(turn * (nz // 2), nz // 2)
        return pltpu.make_async_remote_copy(
            src_ref=part.at[1 - y, core, f, span], dst_ref=yrecv.at[sender, f, span],
            send_sem=ysend_sem.at[f, turn, 0], recv_sem=yrecv_sem.at[f, turn, sender],
            device_id=partner, device_id_type=pl.DeviceIdType.MESH,
        )

    def t_copy(f):
        return pltpu.make_async_remote_copy(
            src_ref=part.at[y, 1 - core, f], dst_ref=trecv.at[f],
            send_sem=tsend_sem.at[f], recv_sem=trecv_sem.at[f],
            device_id=twin, device_id_type=pl.DeviceIdType.MESH,
        )

    def z_copy(f, dz):
        to_z = (z + dz) % nz
        return pltpu.make_async_remote_copy(
            src_ref=zsend.at[f, to_z], dst_ref=zrecv.at[f, dz],
            send_sem=zsend_sem.at[f, dz], recv_sem=zrecv_sem.at[f, dz],
            device_id={"refl": to_z * 2 + y, "freq": core},
            device_id_type=pl.DeviceIdType.MESH,
        )

    def h_copy(turn, dz):
        to_z = (z + dz) % nz
        parity = (y + 1 - turn) % 2
        return pltpu.make_async_remote_copy(
            src_ref=part.at[parity, :, 0, to_z], dst_ref=hrecv.at[turn, dz],
            send_sem=hsend_sem.at[turn, dz], recv_sem=hrecv_sem.at[turn, dz],
            device_id={"refl": to_z * 2 + y, "freq": core},
            device_id_type=pl.DeviceIdType.MESH,
        )

    def l_copy(k):
        to = core if k == 0 else 1 - core
        return pltpu.make_async_remote_copy(
            src_ref=hsum.at[k // 2, to], dst_ref=hlast.at[k],
            send_sem=lsend_sem.at[k], recv_sem=lrecv_sem.at[k],
            device_id=(partner, met[2], twin)[k], device_id_type=pl.DeviceIdType.MESH,
        )

    def products(f):
        real = spec[f, 0, :sources] * jnp.bfloat16(amplitude)
        imag = spec[f, 1, :sources] * jnp.bfloat16(amplitude)
        by_real = jnp.concatenate([real, imag], 0)
        by_imag = jnp.concatenate([-imag, real], 0)
        def one(turn, carry):
            parity = (1 - y) * (1 - turn) + y * turn
            spans = [
                pl.ds(pl.multiple_of((parity + 2 * g) * lanes, lanes), lanes)
                for g in range(2)
            ]
            terms = dot_nt(
                by_real, jnp.concatenate([spec[f, 0, span] for span in spans], 0)
            ) + dot_nt(
                by_imag, jnp.concatenate([spec[f, 1, span] for span in spans], 0)
            )
            for g in range(2):
                for p in range(n_refl // 4):
                    to_z = (4 * p + 2 * g - 2) % n_refl // 2
                    for c in range(2):
                        row = c * sources + p * ts
                        a = terms[row : row + half, g * lanes : (g + 1) * lanes]
                        b = terms[row + half : row + ts, g * lanes : (g + 1) * lanes]
                        turned = pltpu.roll(jnp.where(low, b, a), tr, 1)
                        part[parity, 0, f, to_z, c] = jnp.where(low, a, turned).astype(
                            jnp.bfloat16
                        )
                        part[parity, 1, f, to_z, c] = jnp.where(low, turned, b).astype(
                            jnp.bfloat16
                        )
            @pl.when((turn == 0) & (f == 0))
            def _():
                pl.semaphore_wait(barrier, len(met))

            @pl.when(f == 0)
            def _():
                for dz in range(1, nz):
                    h_copy(turn, dz).start()

            @pl.when((turn == 0) & (f > 0))
            def _():
                for piece in range(2):
                    for other in range(n_freq):
                        y_copy(f, other, piece).start()

            @pl.when((turn == 1) & (f > 0))
            def _():
                t_copy(f).start()

            return carry

        lax.fori_loop(0, 2, one, 0)

    def forward(f):
        t_copy(f).wait_recv()
        for piece in range(2):
            for sender in range(n_freq):
                y_arrival(f, sender, piece).wait_recv()
            span = slice(piece * (nz // 2), (piece + 1) * (nz // 2))
            for owner, block in ((core, part.at[y, core, f]), (1 - core, trecv.at[f])):
                zsend[f, span, owner] = block[span] + yrecv[owner, f, span]
            for to_z in range(piece * (nz // 2), (piece + 1) * (nz // 2)):
                @pl.when(z != to_z)
                def _():
                    z_copy(f, (to_z - z + nz) % nz).start()

    def z_arrival(f, dz):
        return pltpu.make_async_remote_copy(
            src_ref=zsend.at[f, z], dst_ref=zrecv.at[f, dz],
            send_sem=zsend_sem.at[f, dz], recv_sem=zrecv_sem.at[f, dz],
            device_id=partner, device_id_type=pl.DeviceIdType.MESH,
        )

    def gather(f):
        for dz in range(1, nz):
            z_arrival(f, dz).wait_recv()
        summed = zsend[f, z].astype(jnp.float32)
        for dz in range(1, nz):
            summed = summed + zrecv[f, dz].astype(jnp.float32)
        csum[f] = summed.astype(jnp.bfloat16)

    def head():
        for turn in range(2):
            for dz in range(1, nz):
                h_copy(turn, dz).wait_recv()
            summed = part[(y + 1 - turn) % 2, :, 0, z].astype(jnp.float32)
            for dz in range(1, nz):
                summed = summed + hrecv[turn, dz].astype(jnp.float32)
            hsum[turn] = summed.astype(jnp.bfloat16)
            for k in ((0, 1), (2,))[turn]:
                l_copy(k).start()

    def finish():
        for k in range(3):
            l_copy(k).wait_recv()
        for owner, block, k in ((core, hsum.at[1, core], 0), (1 - core, hlast.at[2], 1)):
            csum[0, owner] = (
                block[...].astype(jnp.float32) + hlast[k].astype(jnp.float32)
            ).astype(jnp.bfloat16)

    def absorb(f):
        source = lax.broadcasted_iota(jnp.int32, (half, lanes), 0)
        outer = (low & (source < WM)) | (~low & (source >= half - WM))
        for owner in range(n_freq):
            block = csum[f, owner]
            index = owner * nf + f
            xr = block[0].astype(jnp.float32)
            xi = block[1].astype(jnp.float32)
            d0 = dat[pl.ds(pl.multiple_of(index * half, half), half), :]
            d1 = dat[pl.ds(pl.multiple_of((NF + index) * half, half), half), :]
            sums = (xr * xr + xi * xi, xr * d0 + xi * d1, xi * d0 - xr * d1)
            for k in range(3):
                every[pl.ds(k * NF + index, 1), :] = jnp.sum(sums[k], 0, keepdims=True)
                edge[pl.ds(k * NF + index, 1), :] = jnp.sum(
                    jnp.where(outer, sums[k], 0.0), 0, keepdims=True
                )
            xt[pl.ds(index, half, stride=2 * NF), :] = xr
            xt[pl.ds(NF + index, half, stride=2 * NF), :] = xi

    def steady(f, carry):
        spec_copy(f).wait()

        @pl.when((f > 0) & (f + DEPTH - 1 < nf))
        def _():
            spec_copy(f + DEPTH - 1).start()

        products(f)

        @pl.when(f == min(HEAD, nf - 1))
        def _():
            head()

        @pl.when(f > LAG)
        def _():
            forward(f - LAG)

        @pl.when(f > LAG + ZLAG)
        def _():
            gather(f - LAG - ZLAG)

        return carry

    for copy in side_copies:
        copy.start()
    lax.fori_loop(0, nf, steady, 0)

    for copy in side_copies:
        copy.wait()
    table = tables[0 : 2 * NF].astype(jnp.bfloat16)
    basis = tables[2 * NF : 4 * NF, :TAPS]
    lags = tables[2 * NF : 4 * NF, lanes : lanes + TAPS]
    gram = tables[4 * NF : 6 * NF, : 2 * NF]
    sel = tables[6 * NF : 6 * NF + 24].astype(jnp.bfloat16)
    basis_halves, lags_halves, gram_halves = halves(basis), halves(lags), halves(gram)
    table_ref[...] = table

    def project(s, carry):
        traces = jnp.concatenate([rec[s], rec[half + s]], 0)
        dat[pl.ds(s, 2 * NF, stride=half), :] = dot_nt(table, traces)
        return carry

    lax.fori_loop(0, half, project, 0, unroll=4)
    start = start_ref[...]
    u0 = dot_nt(start, basis, EXACT)

    def absorb_step(f, carry):
        absorb(f)
        return carry

    ready = max(nf - LAG - ZLAG, 1)
    lax.fori_loop(1, ready, absorb_step, 0)

    def drain(f, carry):
        @pl.when(f < nf)
        def _():
            forward(f)

        @pl.when(f - ZLAG >= 1)
        def _():
            gather(f - ZLAG)
            absorb(f - ZLAG)

        @pl.when(f == nf)
        def _():
            finish()
            absorb(0)

        return carry

    lax.fori_loop(nf - LAG, nf + ZLAG, drain, 0)

    tall = jnp.concatenate([every[:NF], every[...]], 0)
    stat[0, :, : 4 * NF] = dot_nt(sel[:8], split(tall))
    tall = jnp.concatenate([edge[:NF], edge[...]], 0)
    edges = dot_nt(sel[8:], split(tall))
    stat[1, :, : 4 * NF] = edges[:8]
    stat[2, :, : 4 * NF] = edges[8:]

    place = (me + 2 * n_freq) % total
    p, q = place // columns, place % columns

    def halo_copy(j):
        slot = offsets.index((total - offsets[j]) % total)
        if offsets[j] in (1, total - 1):
            kind = 0
        else:
            kind = 1 + jnp.where((place + offsets[j]) % total // columns > p, 1, 0)
        return pltpu.make_async_remote_copy(
            src_ref=stat.at[kind], dst_ref=nrecv.at[slot],
            send_sem=nsend_sem.at[j], recv_sem=nrecv_sem.at[slot],
            device_id=device((me + offsets[j]) % total),
            device_id_type=pl.DeviceIdType.MESH,
        )

    copies = [halo_copy(j) for j in range(len(offsets))]
    for copy in copies[1:-1] + [copies[0], copies[-1]]:
        copy.start()

    def settle(f, carry):
        for piece in range(2):
            for other in range(n_freq):
                y_copy(f, other, piece).wait_send()
        t_copy(f).wait_send()
        for dz in range(1, nz):
            z_copy(f, dz).wait_send()
        return carry

    lax.fori_loop(1, nf, settle, 0)
    for turn in range(2):
        for dz in range(1, nz):
            h_copy(turn, dz).wait_send()
    for k in range(3):
        l_copy(k).wait_send()
    for copy in copies:
        copy.wait_recv()

    windows = stat[0, 0:2, : 4 * NF]
    for dp, dq in directions:
        slot = offsets.index((dp * columns + dq) % total)
        first = {-1: 2, 0: 0, 1: 4}[dq]
        inside = (p + dp >= 0) & (p + dp < rows) & (q + dq >= 0) & (q + dq < columns)
        windows = windows + jnp.where(
            inside, nrecv[slot, first : first + 2, : 4 * NF], 0.0
        )

    power = windows[:, : 2 * NF]
    cross = windows[:, 2 * NF : 4 * NF]
    weight = power * ((NT / 2) * (2.0 / NF))
    residual = cross - weight * u0
    lag_gram = dot_halves(power, lags_halves)
    once = dot_halves(residual, gram_halves)
    twice = dot_halves(weight * once, gram_halves)
    tap = lax.broadcasted_iota(jnp.int32, lag_gram.shape, 1)
    bound = jnp.sum(jnp.where(tap == 0, lag_gram, 2.0 * jnp.abs(lag_gram)), 1, keepdims=True)
    step = 0.5 / (bound + 1e-06)
    v = step * (3.0 * residual - step * (weight * (3.0 * once - step * twice)))
    filters = start + dot_halves(v, basis_halves)
    filters_ref[...] = filters
    taps = filters.astype(jnp.bfloat16)
    response = dot_nt(basis_halves[0], taps) + dot_nt(basis_halves[1], taps)
    window_of = lax.broadcasted_iota(jnp.int32, (NF, lanes), 1) % tr < WC
    hc = jnp.where(window_of, response[:NF, 0:1], response[:NF, 1:2])
    hs = jnp.where(window_of, response[NF:, 0:1], response[NF:, 1:2])

    for s in range(half):
        xr = xt[2 * NF * s : 2 * NF * s + NF]
        xi = xt[2 * NF * s + NF : 2 * NF * (s + 1)]
        shaped = jnp.concatenate([xr * hc + xi * hs, xi * hc - xr * hs], 0)
        shaped_ref[s] = shaped.astype(jnp.bfloat16)

    for copy in copies:
        copy.wait_send()


def subtract(
    shaped_ref, filters_ref, rec, table_ref, primaries_hbm, filters_hbm,
    outv, out_sem, filters_sem,
):
    half, tr = shaped_ref.shape[0], rec.shape[1]
    group = half // out_sem.shape[0]
    filters_copy = pltpu.make_async_copy(filters_ref, filters_hbm, filters_sem)
    filters_copy.start()
    copies = []
    for s in range(half):
        predicted = lax.dot_general(
            shaped_ref[s], table_ref[...], (((0,), (0,)), ((), ())),
            preferred_element_type=jnp.float32,
        )
        outv[s] = (rec[s].astype(jnp.float32) - predicted[:tr]).astype(jnp.bfloat16)
        outv[half + s] = (
            rec[half + s].astype(jnp.float32) - predicted[tr:]
        ).astype(jnp.bfloat16)
        if s % group == group - 1:
            for h in range(2):
                span = pl.ds(h * half + s - group + 1, group)
                copy = pltpu.make_async_copy(
                    outv.at[span], primaries_hbm.at[span], out_sem.at[s // group, h]
                )
                copy.start()
                copies.append(copy)
    for copy in copies + [filters_copy]:
        copy.wait()


def body(mesh_shape, spectra, recorded, initial_filters):
    n_refl, n_freq = mesh_shape["refl"], mesh_shape["freq"]
    nf, receivers, points = spectra.shape[1:]
    ts, tr, samples = recorded.shape[2:]
    sources = ts * (n_refl // 4)
    nz = n_refl // 2
    half, lanes = ts // 2, 2 * tr
    total, columns = n_refl * n_freq, 4 * n_freq
    n_halo = len(
        {(dp * columns + dq) % total for dp in (-1, 0, 1) for dq in (-1, 0, 1)} - {0}
    )
    basis, gram, lags = filter_tables()
    vmem = pl.BlockSpec(memory_space=pltpu.VMEM)
    hbm = pl.BlockSpec(memory_space=pltpu.HBM)
    tables = np.zeros((6 * NF + 24, max(samples, 2 * lanes)), np.float32)
    tables[: 2 * NF, :samples] = time_rows().astype(ml_dtypes.bfloat16).astype(np.float32)
    tables[2 * NF : 4 * NF, :TAPS] = basis
    tables[2 * NF : 4 * NF, lanes : lanes + TAPS] = lags
    tables[4 * NF : 6 * NF, : 2 * NF] = gram
    tables[6 * NF :] = lane_selection(tr)
    bf16, f32 = jnp.bfloat16, jnp.float32
    staged = pl.pallas_call(
        functools.partial(kernel, n_refl, n_freq, sources),
        out_shape=(
            jax.ShapeDtypeStruct((half, 2 * NF, lanes), bf16),
            jax.ShapeDtypeStruct((2, TAPS), f32),
            jax.ShapeDtypeStruct((ts, tr, samples), bf16),
            jax.ShapeDtypeStruct((2 * NF, samples), bf16),
        ),
        in_specs=[hbm] * 4,
        out_specs=(vmem,) * 4,
        scratch_shapes=[
            pltpu.VMEM((2, TAPS), f32),
            pltpu.VMEM(tables.shape, f32),
            pltpu.VMEM((nf, 2, receivers, points), bf16),
            pltpu.VMEM((2, n_freq, nf, nz, 2, half, lanes), bf16),
            pltpu.VMEM((n_freq, nf, nz, 2, half, lanes), bf16),
            pltpu.VMEM((nf, nz, 2, half, lanes), bf16),
            pltpu.VMEM((nf, nz, n_freq, 2, half, lanes), bf16),
            pltpu.VMEM((nf, nz, n_freq, 2, half, lanes), bf16),
            pltpu.VMEM((2, nz, n_freq, 2, half, lanes), bf16),
            pltpu.VMEM((2, n_freq, 2, half, lanes), bf16),
            pltpu.VMEM((3, 2, half, lanes), bf16),
            pltpu.VMEM((nf, n_freq, 2, half, lanes), bf16),
            pltpu.VMEM((2 * NF * half, lanes), f32),
            pltpu.VMEM((half * 2 * NF, lanes), f32),
            pltpu.VMEM((3 * NF, lanes), f32),
            pltpu.VMEM((3 * NF, lanes), f32),
            pltpu.VMEM((3, 8, lanes), f32),
            pltpu.VMEM((n_halo, 8, lanes), f32),
            pltpu.SemaphoreType.DMA((nf,)),
            pltpu.SemaphoreType.DMA,
            pltpu.SemaphoreType.DMA,
            pltpu.SemaphoreType.DMA,
            pltpu.SemaphoreType.DMA((nf, 2, n_freq)),
            pltpu.SemaphoreType.DMA((nf, 2, n_freq)),
            pltpu.SemaphoreType.DMA((nf, nz)),
            pltpu.SemaphoreType.DMA((nf, nz)),
            pltpu.SemaphoreType.DMA((nf,)),
            pltpu.SemaphoreType.DMA((nf,)),
            pltpu.SemaphoreType.DMA((2, nz)),
            pltpu.SemaphoreType.DMA((2, nz)),
            pltpu.SemaphoreType.DMA((3,)),
            pltpu.SemaphoreType.DMA((3,)),
            pltpu.SemaphoreType.DMA((n_halo,)),
            pltpu.SemaphoreType.DMA((n_halo,)),
        ],
        compiler_params=pltpu.CompilerParams(
            collective_id=0, has_side_effects=True, vmem_limit_bytes=40 * 1024 * 1024
        ),
    )(
        *[
            pltpu.with_memory_space_constraint(x, pltpu.HBM)
            for x in (
                spectra,
                recorded.reshape(ts, tr, samples),
                initial_filters.reshape(2, TAPS),
                jnp.asarray(tables),
            )
        ]
    )
    primaries, filters = pl.pallas_call(
        subtract,
        out_shape=(
            jax.ShapeDtypeStruct((ts, tr, samples), bf16),
            jax.ShapeDtypeStruct((2, TAPS), f32),
        ),
        in_specs=[vmem] * 4,
        out_specs=(hbm, hbm),
        scratch_shapes=[
            pltpu.VMEM((ts, tr, samples), bf16),
            pltpu.SemaphoreType.DMA((4, 2)),
            pltpu.SemaphoreType.DMA,
        ],
        compiler_params=pltpu.CompilerParams(vmem_limit_bytes=40 * 1024 * 1024),
    )(*staged)
    return (
        primaries.reshape(recorded.shape),
        filters.reshape(initial_filters.shape),
    )


def solution(mesh):
    placed = (
        P(None, "freq", "groups", "refl"),
        P("refl", "freq", "groups", None, None),
        P("refl", "freq", "groups", None, None),
    )
    return jax.shard_map(
        functools.partial(body, dict(mesh.shape)),
        mesh=mesh,
        in_specs=placed,
        out_specs=(
            P("refl", "freq", "groups", None, None),
            P("refl", "freq", "groups", None, None),
        ),
        check_vma=False,
    )
```
